256 devices in a mesh: adapter: 32 (over x, y, core), tensor: 8 (over z).
Axes of the slice: x: 4, y: 4, z: 8, core: 2. Of those that a mesh axis runs over, the one named last changes fastest.
Arguments:
- tokens: bfloat16 [2048, 16384], P('tensor', 'adapter'), may hold values from -6 to 6
- query_weight: bfloat16 [16384, 16384], P('adapter', 'tensor'), may hold values from -0.046875 to 0.046875
- adapter_down_factors: bfloat16 [128, 16, 16384], P('adapter'), may hold values from -0.046875 to 0.046875
- adapter_up_factors: bfloat16 [128, 16, 16384], P('adapter'), may hold values from -0.75 to 0.75
- request_combination: int32 [2048], replicated, may hold values from 0 to 511, as said below
- combination_task_ids: int32 [512, 4], replicated, may hold values from 0 to 127, as said below
- combination_coefficient: int32 [512, 4], replicated, may hold values from -4 to 4
Outputs:
- query: bfloat16 [2048, 16384], P('adapter', 'tensor')
The draws below stay inside these ranges and needn't reach their ends.
Inputs may be any that keep to these rules, and one draw needn't show every extreme that they name: `request_combination`: combination c belongs to owner c // 16. In each aligned block of 256 requests at most 32 requests name combinations of one owner, and one owner, the same for every block, has exactly 32 in every block. `combination_task_ids`: every entry of row c names a task vector of (c // 16) * 4 to (c // 16) * 4 + 3.
All inputs are finite; a program needn't handle non-finite values.
Results may differ from the reference program's by a relative error of at most 0.0042.
Values may be sent and summed in bfloat16 or wider, within the bound.
A program may use at most 128 MiB of HBM per device.

```python
import jax
import jax.numpy as jnp
from jax import lax

MODEL_WIDTH = 16384
QUERY_FEATURES = 16384
TASK_RANK = 16
TERMS = 4
TASKS_PER_SHARD = 4
COMBO_DEV = 16
REQUESTS = 2048
TASK_TOTAL = 128
COMBOS = 512
BLOCK_ROWS = 256
CAP = 32
N_ADAPTER = 32
N_TENSOR = 8


def draw_request_combination(key, part):
    key_hot, key_rest = jax.random.split(key)
    hot_owner = jax.random.randint(key_hot, (), 0, N_ADAPTER).astype(jnp.int32)
    block_keys = jax.random.split(key_rest, N_TENSOR)

    def one_block(block_key):
        key_slot, key_rows, key_local = jax.random.split(block_key, 3)
        slot_order = jax.random.permutation(key_slot, (N_ADAPTER - 1) * CAP)[:BLOCK_ROWS - CAP]
        others = (slot_order // CAP).astype(jnp.int32)
        others = others + (others >= hot_owner).astype(jnp.int32)
        owners = jnp.concatenate([jnp.full((CAP,), 1, jnp.int32) * hot_owner, others])
        owners = owners[jax.random.permutation(key_rows, BLOCK_ROWS)]
        local_combo = jax.random.randint(key_local, (BLOCK_ROWS,), 0, COMBO_DEV).astype(jnp.int32)
        return owners * COMBO_DEV + local_combo
    return jax.vmap(one_block)(block_keys).reshape(-1).astype(jnp.int32)


def draw_combination_task_ids(key, part):
    owner = (jnp.arange(COMBOS, dtype=jnp.int32) // COMBO_DEV).astype(jnp.int32)
    local_task = jax.random.randint(key, (COMBOS, TERMS), 0, TASKS_PER_SHARD).astype(jnp.int32)
    return (owner[:, None] * TASKS_PER_SHARD + local_task).astype(jnp.int32)


def plant(array, stream_key, least, high):
    extent = array.shape
    place = [jax.random.randint(jax.random.fold_in(stream_key, axis), (), 0, extent[axis]) for axis in range(len(extent))]
    array = array.at[tuple(place)].set(least)
    longest = extent.index(max(extent))
    place[longest] = (place[longest] + 1) % extent[longest]
    return array.at[tuple(place)].set(high)


def block_scale(key, extent, pieces, low, top_value):
    loudness = 1.0
    for axis_at, parts in pieces:
        draws = jax.random.uniform(jax.random.fold_in(jax.random.fold_in(key, 6), axis_at), (parts,), jnp.float32, low / len(pieces), top_value / len(pieces))
        loudness = loudness * jnp.repeat(jnp.exp(draws), extent[axis_at] // parts).reshape((-1,) + (1,) * (len(extent) - 1 - axis_at))
    return loudness


def centred(rng, shape, spread, most, pieces=(), kind=jnp.bfloat16):
    drawn = spread * jax.random.normal(rng, shape, jnp.float32)
    if pieces:
        drawn = drawn * block_scale(rng, shape, pieces, -0.22, 0.18)
    return jnp.clip(drawn, -most, most).astype(kind)


def setup_inputs(seed: int = 0) -> dict:
    arg_keys = jax.random.split(jax.random.key(seed), 8)
    return {
        "tokens": centred(arg_keys[0], (REQUESTS, MODEL_WIDTH), 1.0, 6.0, ((0, 8), (1, 32))),
        "query_weight": centred(arg_keys[1], (MODEL_WIDTH, QUERY_FEATURES), MODEL_WIDTH ** -0.5, 0.046875, ((0, 32), (1, 8))),
        "adapter_down_factors": centred(arg_keys[2], (TASK_TOTAL, TASK_RANK, MODEL_WIDTH), MODEL_WIDTH ** -0.5, 0.046875, ((0, 32),)),
        "adapter_up_factors": centred(arg_keys[3], (TASK_TOTAL, TASK_RANK, QUERY_FEATURES), (TASKS_PER_SHARD * TASK_RANK) ** -0.5, 0.75, ((0, 32),)),
        "request_combination": draw_request_combination(jax.random.fold_in(arg_keys[7], 71), 0),
        "combination_task_ids": draw_combination_task_ids(jax.random.fold_in(arg_keys[7], 71), 0),
        "combination_coefficient": plant(jax.random.randint(arg_keys[6], (COMBOS, TERMS), -4, 5), jax.random.fold_in(arg_keys[6], 1), -4, 4).astype(jnp.int32),
    }


def reference(tokens, query_weight, adapter_down_factors, adapter_up_factors, request_combination, combination_task_ids, combination_coefficient):
    base = jnp.dot(tokens, query_weight, preferred_element_type=jnp.float32)
    owner = (request_combination // COMBO_DEV).astype(jnp.int32)
    tasks_of = combination_task_ids[request_combination]
    coef_of = combination_coefficient[request_combination].astype(jnp.float32)
    local_ids = owner[:, None] * TASKS_PER_SHARD + jnp.arange(TASKS_PER_SHARD, dtype=jnp.int32)[None, :]
    hits = (tasks_of[:, :, None] == local_ids[:, None, :]).astype(jnp.float32)
    weight = 0.25 * jnp.sum(coef_of[:, :, None] * hits, axis=1)
    down_factors_full = adapter_down_factors.reshape(N_ADAPTER, TASKS_PER_SHARD, TASK_RANK, MODEL_WIDTH)
    up_factors_full = adapter_up_factors.reshape(N_ADAPTER, TASKS_PER_SHARD, TASK_RANK, QUERY_FEATURES)
    blocks = REQUESTS // 16

    def one_block(packed):
        tok_block, own_block, weight_block = packed
        down = down_factors_full[own_block].astype(jnp.float32)
        query_output = jnp.einsum("bd,btrd->btr", tok_block.astype(jnp.float32), down)
        scaled_low = (query_output * weight_block[:, :, None]).astype(jnp.bfloat16)
        up = up_factors_full[own_block].astype(jnp.float32)
        delta_rows = jnp.einsum("btr,btrq->bq", scaled_low.astype(jnp.float32), up)
        return delta_rows.astype(jnp.bfloat16)

    delta = lax.map(one_block, (tokens.reshape(blocks, 16, MODEL_WIDTH), owner.reshape(blocks, 16), weight.reshape(blocks, 16, TASKS_PER_SHARD)))
    delta = delta.reshape(REQUESTS, QUERY_FEATURES)
    return (base + delta.astype(jnp.float32)).astype(jnp.bfloat16)
```

```python
import jax
import jax.numpy as jnp
from jax import lax
from jax.experimental import pallas as pl
from jax.experimental.pallas import tpu as pltpu
from jax.sharding import PartitionSpec as P

NX, NY, NZ = 4, 4, 8
NS = 1
RS = 64 // NS
KC = 512
HALF = 1024
QUART = 512
TILE = 256
F32 = jnp.float32
BF16 = jnp.bfloat16


def kernel(
    tok_hbm, w_hbm, a_hbm, b_hbm, rows_ref, ids_ref, coef_ref,
    out_ref,
    tok, wf, a1, a2, bx, by,
    own_n, low_n, lt, lx, ly, low_own, low_all,
    s2, r2, s1, r1, acc, t2, q2, t1, q1,
    send_sem, recv_sem, local_sem,
):
    a_idx = lax.axis_index("adapter")
    z = lax.axis_index("tensor")
    x = a_idx // 8
    y = (a_idx // 2) % 4
    c = a_idx % 2
    other = 1 - c

    def dev(xx, yy, cc, zz):
        return {"adapter": (xx * 4 + yy) * 2 + cc, "tensor": zz}

    def x_peer(k):
        return dev((x + k) % 4, y, c, z)

    def y_peer(k):
        return dev(x, (y + k) % 4, c, z)

    def z_peer(k):
        return dev(x, y, c, (z + k) % 8)

    partner = dev(x, y, other, z)

    counter = [0, 0]

    def remote(src, dst, device):
        i = counter[0]
        counter[0] += 1
        return pltpu.make_async_remote_copy(
            src, dst, send_sem.at[i], recv_sem.at[i],
            device_id=device, device_id_type=pl.DeviceIdType.MESH,
        )

    def local(src, dst):
        i = counter[1]
        counter[1] += 1
        return pltpu.make_async_copy(src, dst, local_sem.at[i])

    sent = []

    def go(copy):
        copy.start()
        sent.append(copy)
        return copy

    my_cols = pl.ds(pl.multiple_of(c * KC, KC), KC)
    tok_local = [
        local(tok_hbm.at[jj, c, s], tok.at[s, 2 * z + jj, :, my_cols])
        for s in range(NS) for jj in range(2)
    ]
    for cp in tok_local:
        cp.start()
    w_local = local(w_hbm, wf.at[my_cols, :])
    w_local.start()
    b_cols = [pl.ds(pl.multiple_of(z * 2048 + h * HALF, HALF), HALF) for h in range(2)]
    b_local = [
        local(b_hbm.at[:, b_cols[0]], bx.at[c, x]),
        local(b_hbm.at[:, b_cols[1]], by.at[c, y]),
    ]
    for cp in b_local:
        cp.start()
    a_wide = lambda xx: pl.ds(pl.multiple_of(xx * 4096, 4096), 4096)
    a_local = local(a_hbm.at[z, :, a_wide(x)], a1.at[x])
    a_local.start()

    barrier = pltpu.get_barrier_semaphore()
    peers = [partner]
    peers += [x_peer(k) for k in range(1, 4)] + [y_peer(k) for k in range(1, 4)]
    peers += [z_peer(k) for k in range(1, 8)]
    for peer in peers:
        pl.semaphore_signal(barrier, inc=1, device_id=peer, device_id_type=pl.DeviceIdType.MESH)
    pl.semaphore_wait(barrier, len(peers))

    tok_pre = [
        go(remote(tok_hbm.at[jj, other, s], tok.at[s, 2 * z + jj, :, my_cols], partner))
        for s in range(NS) for jj in range(2)
    ]
    a_x = [go(remote(a_hbm.at[z, :, a_wide((x + k) % 4)], a1.at[x], x_peer(k))) for k in range(1, 4)]
    w_pre = go(remote(w_hbm, wf.at[my_cols, :], partner))
    b_x = [go(remote(b_hbm.at[:, b_cols[0]], bx.at[c, x], x_peer(k))) for k in range(1, 4)]
    b_y = [go(remote(b_hbm.at[:, b_cols[1]], by.at[c, y], y_peer(k))) for k in range(1, 4)]

    for cp in tok_local:
        cp.wait()
    for cp in tok_pre:
        cp.wait_recv()

    def ring_start(s, k):
        right = (z - k + 8) % 8
        left = (z + k) % 8
        if k < 3:
            src_r = tok.at[s, pl.ds(2 * right, 2)]
            src_l = tok.at[s, pl.ds(2 * left, 2)]
        else:
            src_r = tok.at[s, 2 * right]
            src_l = tok.at[s, 2 * left + 1]
        return go(remote(src_r, src_r, z_peer(1))), go(remote(src_l, src_l, z_peer(7)))

    def ring_wait(pair):
        pair[0].wait_recv()
        pair[1].wait_recv()

    pair = ring_start(0, 0)

    combo = lax.broadcasted_iota(jnp.int32, (512, 4), 0)
    hit = (ids_ref[...] - (combo // 16) * 4) == (z // 2)
    table = 0.25 * jnp.sum(jnp.where(hit, coef_ref[...], 0).astype(F32), axis=1, keepdims=True)
    rows = rows_ref[...]
    weight = jnp.concatenate(
        [
            jnp.sum(
                jnp.where(
                    lax.broadcasted_iota(jnp.int32, (512, 128), 0) == rows[:, 128 * k:128 * (k + 1)],
                    table, 0.0,
                ),
                axis=0, keepdims=True,
            )
            for k in range(8)
        ],
        axis=1,
    )
    owner = rows // 16
    owner_f = owner.astype(F32)
    for k in range(8):
        tile = jnp.broadcast_to(owner_f[:, 128 * k:128 * (k + 1)], (128, 128))
        own_n[128 * k:128 * (k + 1), :] = jnp.transpose(tile)

    a_local.wait()
    for cp in a_x:
        cp.wait_recv()
    a_narrow = lambda yy: pl.ds(pl.multiple_of(yy * 1024, 1024), 1024)
    a_own = local(a1.at[:, :, a_narrow(y)], a2.at[c, y])
    a_own.start()
    a_y = [go(remote(a1.at[:, :, a_narrow((y + k) % 4)], a2.at[c, y], y_peer(k))) for k in range(1, 4)]

    ring_wait(pair)
    pair = ring_start(0, 1)
    a_own.wait()
    for cp in a_y:
        cp.wait_recv()
    a_c = go(remote(a2.at[c], a2.at[c], partner))
    for cp in b_local:
        cp.wait()
    for cp in b_x + b_y:
        cp.wait_recv()
    b_c = [go(remote(bx.at[c], bx.at[c], partner)), go(remote(by.at[c], by.at[c], partner))]
    ring_wait(pair)
    pair = ring_start(0, 2)
    w_local.wait()
    w_pre.wait_recv()
    a_c.wait_recv()
    ring_wait(pair)
    pair = ring_start(0, 3)
    ring_wait(pair)

    af = a2[...].reshape(256, 1024)

    def low_tile(k):
        part = lax.dot_general(
            af, tok[0, 4 * k:4 * (k + 1)].reshape(TILE, 1024), (((1,), (1,)), ((), ())),
            preferred_element_type=F32,
        )
        mine = owner[:, TILE * k:TILE * (k + 1)]
        total = jnp.zeros((8, TILE), F32)
        for g in range(32):
            o = ((g % 4) * 4 + (g // 4) % 4) * 2 + g // 16
            total += jnp.where(mine == o, part[8 * g:8 * (g + 1)], 0.0)
        return total

    for k in range(4):
        lt[:, TILE * k:TILE * (k + 1)] = low_tile(k)
    lo_x = [go(remote(lt, lx.at[k - 1], x_peer(k))) for k in range(1, 4)]

    place = (x, y)
    ring_peer = (x_peer, y_peer)

    def chunk_rows(h, q):
        if h == 0:
            return tok[0, pl.ds(4 * q, 4)].reshape(4 * RS, 1024)
        return jnp.concatenate([tok[0, 4 * j + q] for j in range(4)], axis=0)

    def dots(h, q, first, count, emit):
        lhs = chunk_rows(h, q)
        for n in range(first, first + count):
            cols = slice(h * HALF + n * TILE, h * HALF + (n + 1) * TILE)
            emit(n, jnp.dot(lhs, wf[:, cols], preferred_element_type=F32))

    def cut(n):
        return slice(n * TILE, (n + 1) * TILE)

    lo, hi = pl.ds(0, QUART), pl.ds(QUART, QUART)
    m2 = []
    for h in range(2):
        def put(n, v, h=h):
            s2[h, :, cut(n)] = v.astype(BF16)
        dots(h, (place[h] + 2) % 4, 0, 4, put)
        m2.append((
            go(remote(s2.at[h, :, lo], r2.at[h, 0], ring_peer[h](1))),
            go(remote(s2.at[h, :, hi], r2.at[h, 1], ring_peer[h](3))),
        ))
    m1 = []
    for h in range(2):
        def put_r(n, v, h=h):
            s1[h, 0, :, cut(n)] = v.astype(BF16)
        def put_l(n, v, h=h):
            s1[h, 1, :, cut(n)] = v.astype(BF16)
        dots(h, (place[h] + 1) % 4, 2, 2, put_r)
        m1.append(go(remote(s1.at[h, 0, :, hi], r1.at[h, 0, :, hi], ring_peer[h](1))))
        dots(h, (place[h] + 3) % 4, 0, 2, put_l)
        m1.append(go(remote(s1.at[h, 1, :, lo], r1.at[h, 1, :, lo], ring_peer[h](3))))

    for cp in lo_x:
        cp.wait_recv()
    for cp in lo_x:
        cp.wait_send()
    low_own[...] = (lt[...] + lx[0]) + (lx[1] + lx[2])
    lo_y = [go(remote(low_own, ly.at[k - 1], y_peer(k))) for k in range(1, 4)]

    for h in range(2):
        def keep(n, v, h=h):
            acc[h, :, cut(n)] = v
        dots(h, place[h], 0, 4, keep)
    for h in range(2):
        m2[h][0].wait_recv()
        m2[h][1].wait_recv()
        def add_r(n, v, h=h):
            s1[h, 0, :, cut(n)] = (v + r2[h, 0, :, cut(n)].astype(F32)).astype(BF16)
        def add_l(n, v, h=h):
            s1[h, 1, :, cut(n)] = (v + r2[h, 1, :, cut(n - 2)].astype(F32)).astype(BF16)
        dots(h, (place[h] + 1) % 4, 0, 2, add_r)
        m1.append(go(remote(s1.at[h, 0, :, lo], r1.at[h, 0, :, lo], ring_peer[h](1))))
        dots(h, (place[h] + 3) % 4, 2, 2, add_l)
        m1.append(go(remote(s1.at[h, 1, :, hi], r1.at[h, 1, :, hi], ring_peer[h](3))))

    for cp in lo_y:
        cp.wait_recv()
    total = (low_own[...] + ly[0]) + (ly[1] + ly[2])
    low_all[z] = (total * weight).astype(BF16)
    lo_z = [go(remote(low_all.at[z], low_all.at[z], z_peer(k))) for k in range(1, 8)]
    for cp in lo_z:
        cp.wait_recv()
    low_t = low_all[...].astype(F32).reshape(64, 1024)
    for k in range(8):
        tile = low_t[:, 128 * k:128 * (k + 1)]
        low_n[128 * k:128 * (k + 1), :] = jnp.transpose(jnp.concatenate([tile, tile], axis=0))

    for cp in b_c:
        cp.wait_recv()
    for cp in m1:
        cp.wait_recv()
    lane = lax.broadcasted_iota(jnp.int32, (4 * RS, 128), 1)

    def masked(h):
        if h == 0:
            at = pl.ds(pl.multiple_of(x * 4 * RS, 4 * RS), 4 * RS)
            ow, lw = own_n[at, :], low_n[at, :]
        else:
            ats = [pl.ds(pl.multiple_of((4 * j + y) * RS, RS), RS) for j in range(4)]
            ow = jnp.concatenate([own_n[at, :] for at in ats], axis=0)
            lw = jnp.concatenate([low_n[at, :] for at in ats], axis=0)
        pieces = []
        for cc in range(2):
            for m in range(2):
                if h == 0:
                    o0, step = ((2 * m) * 4 + y) * 2 + cc, 8
                else:
                    o0, step = (x * 4 + 2 * m) * 2 + cc, 2
                want = jnp.where(lane < 64, o0, o0 + step).astype(F32)
                pieces.append(jnp.where(ow == want, lw, 0.0).astype(BF16))
        return jnp.concatenate(pieces, axis=1)

    for h in range(2):
        lhs = masked(h)
        up = (bx, by)[h]
        for n in range(4):
            delta = jnp.dot(
                lhs, up[:, :, :, cut(n)].reshape(512, TILE), preferred_element_type=F32
            )
            acc[h, :, cut(n)] = (acc[h, :, cut(n)] + delta) + (
                r1[h, 0, :, cut(n)].astype(F32) + r1[h, 1, :, cut(n)].astype(F32)
            )

    place2 = (y, x)
    peer2 = (y_peer, x_peer)

    def block(h, q):
        return pl.ds(pl.multiple_of(q * RS, RS), RS)

    n2, n1 = [], []
    for h in range(2):
        t2[h] = acc[h, block(h, (place2[h] + 2) % 4), :].astype(BF16)
        n2.append((
            go(remote(t2.at[h, :, lo], q2.at[h, 0], peer2[h](1))),
            go(remote(t2.at[h, :, hi], q2.at[h, 1], peer2[h](3))),
        ))
    for h in range(2):
        t1[h, 0, :, QUART:] = acc[h, block(h, (place2[h] + 1) % 4), QUART:].astype(BF16)
        n1.append(go(remote(t1.at[h, 0, :, hi], q1.at[h, 0, :, hi], peer2[h](1))))
        t1[h, 1, :, :QUART] = acc[h, block(h, (place2[h] + 3) % 4), :QUART].astype(BF16)
        n1.append(go(remote(t1.at[h, 1, :, lo], q1.at[h, 1, :, lo], peer2[h](3))))
    for h in range(2):
        n2[h][0].wait_recv()
        n2[h][1].wait_recv()
        t1[h, 0, :, :QUART] = (
            acc[h, block(h, (place2[h] + 1) % 4), :QUART] + q2[h, 0].astype(F32)
        ).astype(BF16)
        n1.append(go(remote(t1.at[h, 0, :, lo], q1.at[h, 0, :, lo], peer2[h](1))))
        t1[h, 1, :, QUART:] = (
            acc[h, block(h, (place2[h] + 3) % 4), QUART:] + q2[h, 1].astype(F32)
        ).astype(BF16)
        n1.append(go(remote(t1.at[h, 1, :, hi], q1.at[h, 1, :, hi], peer2[h](3))))
    for cp in n1:
        cp.wait_recv()
    for h in range(2):
        out_ref[:, h * HALF:(h + 1) * HALF] = (
            acc[h, block(h, place2[h]), :] + (q1[h, 0].astype(F32) + q1[h, 1].astype(F32))
        ).astype(BF16)
    for cp in sent:
        if all(cp is not done for done in lo_x):
            cp.wait_send()


def body(tokens, query_weight, down, up, request_combination, task_ids, coefficient):
    c = lax.axis_index("adapter") % 2
    rows = lax.dynamic_index_in_dim(
        request_combination.reshape(16, 2, NS, RS), c, 1, keepdims=False
    )
    rows = rows.transpose(1, 0, 2).reshape(1, 1024)
    hbm = pl.BlockSpec(memory_space=pl.ANY)
    vmem = pl.BlockSpec(memory_space=pltpu.VMEM)
    n_sem = 96
    return pl.pallas_call(
        kernel,
        out_shape=jax.ShapeDtypeStruct((64, 2048), BF16),
        in_specs=[hbm, hbm, hbm, hbm, vmem, vmem, vmem],
        out_specs=vmem,
        scratch_shapes=[
            pltpu.VMEM((NS, 16, RS, 1024), BF16),
            pltpu.VMEM((1024, 2048), BF16),
            pltpu.VMEM((4, 8, 4096), BF16),
            pltpu.VMEM((2, 4, 4, 8, 1024), BF16),
            pltpu.VMEM((2, 4, 64, HALF), BF16),
            pltpu.VMEM((2, 4, 64, HALF), BF16),
            pltpu.VMEM((1024, 128), F32),
            pltpu.VMEM((1024, 128), F32),
            pltpu.VMEM((8, 1024), F32),
            pltpu.VMEM((3, 8, 1024), F32),
            pltpu.VMEM((3, 8, 1024), F32),
            pltpu.VMEM((8, 1024), F32),
            pltpu.VMEM((8, 8, 1024), BF16),
            pltpu.VMEM((2, 4 * RS, HALF), BF16),
            pltpu.VMEM((2, 2, 4 * RS, QUART), BF16),
            pltpu.VMEM((2, 2, 4 * RS, HALF), BF16),
            pltpu.VMEM((2, 2, 4 * RS, HALF), BF16),
            pltpu.VMEM((2, 4 * RS, HALF), F32),
            pltpu.VMEM((2, RS, HALF), BF16),
            pltpu.VMEM((2, 2, RS, QUART), BF16),
            pltpu.VMEM((2, 2, RS, HALF), BF16),
            pltpu.VMEM((2, 2, RS, HALF), BF16),
            pltpu.SemaphoreType.DMA((n_sem,)),
            pltpu.SemaphoreType.DMA((n_sem,)),
            pltpu.SemaphoreType.DMA((16,)),
        ],
        compiler_params=pltpu.CompilerParams(
            collective_id=0, has_side_effects=True, vmem_limit_bytes=48 * 1024 * 1024
        ),
    )(
        tokens.reshape(2, 2, NS, RS, KC),
        query_weight,
        down.reshape(8, 8, 16384),
        up.reshape(64, 16384),
        rows,
        task_ids,
        coefficient,
    )


def solution(mesh):
    placed = (
        P("tensor", "adapter"),
        P("adapter", "tensor"),
        P("adapter", None, None),
        P("adapter", None, None),
        P(),
        P(),
        P(),
    )
    return jax.shard_map(
        body, mesh=mesh, in_specs=placed, out_specs=P("adapter", "tensor"), check_vma=False
    )
```

```python
import jax
import jax.numpy as jnp
from jax import lax
from jax.experimental import pallas as pl
from jax.experimental.pallas import tpu as pltpu
from jax.sharding import PartitionSpec as P

NS = 2
RS = 64 // NS
SR = 16 * RS
CR = 4 * RS
KC = 512
HALF = 1024
QUART = 512
TILE = 256
F32 = jnp.float32
BF16 = jnp.bfloat16


def kernel(
    tok_hbm, w_hbm, a_hbm, b_hbm, rows_ref, ids_ref, coef_ref,
    out_ref,
    tok, wf, a1, a2, bx, by,
    own_n, low_n, lt, lx, ly, low_own, low_all,
    s2, r2, s1, r1, acc, t2, q2, t1, q1,
    send_sem, recv_sem, local_sem,
):
    a_idx = lax.axis_index("adapter")
    z = lax.axis_index("tensor")
    x = a_idx // 8
    y = (a_idx // 2) % 4
    c = a_idx % 2
    other = 1 - c

    def dev(xx, yy, cc, zz):
        return {"adapter": (xx * 4 + yy) * 2 + cc, "tensor": zz}

    def x_peer(k):
        return dev((x + k) % 4, y, c, z)

    def y_peer(k):
        return dev(x, (y + k) % 4, c, z)

    def z_peer(k):
        return dev(x, y, c, (z + k) % 8)

    partner = dev(x, y, other, z)
    counter = [0, 0]
    sent = []

    def go(src, dst, device):
        i = counter[0]
        counter[0] += 1
        copy = pltpu.make_async_remote_copy(
            src, dst, send_sem.at[i], recv_sem.at[i],
            device_id=device, device_id_type=pl.DeviceIdType.MESH,
        )
        copy.start()
        sent.append(copy)
        return copy

    def local(src, dst):
        i = counter[1]
        counter[1] += 1
        copy = pltpu.make_async_copy(src, dst, local_sem.at[i])
        copy.start()
        return copy

    def arrived(copies):
        for cp in copies:
            cp.wait_recv()

    my_cols = pl.ds(pl.multiple_of(c * KC, KC), KC)
    tok_local = [
        local(tok_hbm.at[jj, c, s], tok.at[s, 2 * z + jj, :, my_cols])
        for s in range(NS) for jj in range(2)
    ]
    a_wide = lambda xx: pl.ds(pl.multiple_of(xx * 4096, 4096), 4096)
    a_narrow = lambda yy: pl.ds(pl.multiple_of(yy * 1024, 1024), 1024)
    a_local = local(a_hbm.at[z, :, a_wide(x)], a1.at[x])
    b_cols = [pl.ds(pl.multiple_of(z * 2048 + h * HALF, HALF), HALF) for h in range(2)]
    b_local = [
        local(b_hbm.at[:, b_cols[0]], bx.at[c, x]),
        local(b_hbm.at[:, b_cols[1]], by.at[c, y]),
    ]
    w_local = local(w_hbm, wf.at[my_cols, :])

    barrier = pltpu.get_barrier_semaphore()
    peers = [partner]
    peers += [x_peer(k) for k in range(1, 4)] + [y_peer(k) for k in range(1, 4)]
    peers += [z_peer(k) for k in range(1, 8)]
    for peer in peers:
        pl.semaphore_signal(barrier, inc=1, device_id=peer, device_id_type=pl.DeviceIdType.MESH)

    lane8 = lax.broadcasted_iota(jnp.int32, (8, 128), 1)
    per = 128 // RS
    groups = []
    for s in range(NS):
        for g in range(16 // per):
            piece = jnp.zeros((8, 128), jnp.int32)
            for j in range(per):
                d = per * g + j
                raw = jnp.broadcast_to(rows_ref[:, 128 * d:128 * (d + 1)], (8, 128))
                shift = (RS * j - RS * s + 256 - 64 * c) % 128
                piece = jnp.where(lane8 // RS == j, pltpu.roll(raw, shift, 1), piece)
            groups.append(piece[0:1])

    combo = lax.broadcasted_iota(jnp.int32, (4, 512), 1)
    hit = (ids_ref[...] - (combo // 16) * 4) == (z // 2)
    table = 0.25 * jnp.sum(jnp.where(hit, coef_ref[...], 0).astype(F32), axis=0, keepdims=True)
    column = jnp.concatenate(
        [
            jnp.transpose(jnp.broadcast_to(table[:, 128 * k:128 * (k + 1)], (128, 128)))
            for k in range(4)
        ],
        axis=0,
    )
    number = lax.broadcasted_iota(jnp.int32, (512, 128), 0)
    weight = jnp.concatenate(
        [
            jnp.sum(jnp.where(number == g, column, 0.0), axis=0, keepdims=True)
            for g in groups
        ],
        axis=1,
    )
    rows = jnp.concatenate(groups, axis=1)
    owner = rows // 16
    owner_f = owner.astype(F32)
    for k in range(8):
        tile = jnp.broadcast_to(owner_f[:, 128 * k:128 * (k + 1)], (128, 128))
        own_n[128 * k:128 * (k + 1), :] = jnp.transpose(tile)

    pl.semaphore_wait(barrier, len(peers))

    tok_pre = [
        go(tok_hbm.at[jj, other, s], tok.at[s, 2 * z + jj, :, my_cols], partner)
        for s in range(NS) for jj in range(2)
    ]
    a_x = [go(a_hbm.at[z, :, a_wide((x + k) % 4)], a1.at[x], x_peer(k)) for k in range(1, 4)]
    w_pre = go(w_hbm, wf.at[my_cols, :], partner)
    b_x = [go(b_hbm.at[:, b_cols[0]], bx.at[c, x], x_peer(k)) for k in range(1, 4)]
    b_y = [go(b_hbm.at[:, b_cols[1]], by.at[c, y], y_peer(k)) for k in range(1, 4)]

    moving = {}

    def ring(s, k):
        for u in range(2):
            ways = ("r", "l") if k < 3 else (("r",), ("l",))[u]
            for way in ways:
                if k > 0:
                    moving.pop((s, k - 1, u, way)).wait_recv()
                b = (z - k + 8) % 8 if way == "r" else (z + k) % 8
                src = tok.at[s, 2 * b + u]
                moving[s, k, u, way] = go(src, src, z_peer(1 if way == "r" else 7))

    def ring_end(s):
        for key in [key for key in moving if key[0] == s]:
            moving.pop(key).wait_recv()

    def low_part(s):
        af = a2[...].reshape(256, 1024)
        for k in range(SR // TILE):
            nd = TILE // RS
            part = lax.dot_general(
                af, tok[s, nd * k:nd * (k + 1)].reshape(TILE, 1024),
                (((1,), (1,)), ((), ())), preferred_element_type=F32,
            )
            mine = owner[:, s * SR + TILE * k:s * SR + TILE * (k + 1)]
            total = jnp.zeros((8, TILE), F32)
            for g in range(32):
                o = ((g % 4) * 4 + (g // 4) % 4) * 2 + g // 16
                total += jnp.where(mine == o, part[8 * g:8 * (g + 1)], 0.0)
            lt[s, :, TILE * k:TILE * (k + 1)] = total
        return [go(lt.at[s], lx.at[s, k - 1], x_peer(k)) for k in range(1, 4)]

    def low_x(s, copies):
        arrived(copies)
        low_own[s] = (lt[s] + lx[s, 0]) + (lx[s, 1] + lx[s, 2])
        return [go(low_own.at[s], ly.at[s, k - 1], y_peer(k)) for k in range(1, 4)]

    def low_y(s, copies):
        arrived(copies)
        total = (low_own[s] + ly[s, 0]) + (ly[s, 1] + ly[s, 2])
        low_all[s, z] = (total * weight[:, s * SR:(s + 1) * SR]).astype(BF16)
        return [go(low_all.at[s, z], low_all.at[s, z], z_peer(k)) for k in (4, 3, 5, 2, 6, 1, 7)]

    def low_z(s, copies):
        arrived(copies)
        low_t = low_all[s].astype(F32).reshape(64, SR)
        for k in range(SR // 128):
            tile = low_t[:, 128 * k:128 * (k + 1)]
            low_n[s * SR + 128 * k:s * SR + 128 * (k + 1), :] = jnp.transpose(
                jnp.concatenate([tile, tile], axis=0)
            )

    place = (x, y)
    ring_peer = (x_peer, y_peer)

    def cut(n):
        return slice(n * TILE, (n + 1) * TILE)

    lo, hi = pl.ds(0, QUART), pl.ds(QUART, QUART)

    def dots(s, h, q, first, count, emit):
        if h == 0:
            lhs = tok[s, pl.ds(4 * q, 4)].reshape(CR, 1024)
        else:
            lhs = jnp.concatenate([tok[s, 4 * j + q] for j in range(4)], axis=0)
        for n in range(first, first + count):
            cols = slice(h * HALF + n * TILE, h * HALF + (n + 1) * TILE)
            emit(n, jnp.dot(lhs, wf[:, cols], preferred_element_type=F32))

    def far(s):
        out = []
        for h in range(2):
            def put(n, v, h=h):
                s2[s, h, :, cut(n)] = v.astype(BF16)
            dots(s, h, (place[h] + 2) % 4, 0, 4, put)
            out.append(go(s2.at[s, h, :, lo], r2.at[s, h, 0], ring_peer[h](1)))
            out.append(go(s2.at[s, h, :, hi], r2.at[s, h, 1], ring_peer[h](3)))
        return out

    def near(s):
        out = []
        for h in range(2):
            def put_r(n, v, h=h):
                s1[s, h, 0, :, cut(n)] = v.astype(BF16)
            def put_l(n, v, h=h):
                s1[s, h, 1, :, cut(n)] = v.astype(BF16)
            dots(s, h, (place[h] + 1) % 4, 2, 2, put_r)
            out.append(go(s1.at[s, h, 0, :, hi], r1.at[s, h, 0, :, hi], ring_peer[h](1)))
            dots(s, h, (place[h] + 3) % 4, 0, 2, put_l)
            out.append(go(s1.at[s, h, 1, :, lo], r1.at[s, h, 1, :, lo], ring_peer[h](3)))
        return out

    def keep(s):
        for h in range(2):
            def put(n, v, h=h):
                acc[s, h, :, cut(n)] = v
            dots(s, h, place[h], 0, 4, put)

    def relay(s, copies):
        out = []
        for h in range(2):
            arrived(copies[2 * h:2 * h + 2])
            def add_r(n, v, h=h):
                s1[s, h, 0, :, cut(n)] = (v + r2[s, h, 0, :, cut(n)].astype(F32)).astype(BF16)
            def add_l(n, v, h=h):
                s1[s, h, 1, :, cut(n)] = (v + r2[s, h, 1, :, cut(n - 2)].astype(F32)).astype(BF16)
            dots(s, h, (place[h] + 1) % 4, 0, 2, add_r)
            out.append(go(s1.at[s, h, 0, :, lo], r1.at[s, h, 0, :, lo], ring_peer[h](1)))
            dots(s, h, (place[h] + 3) % 4, 2, 2, add_l)
            out.append(go(s1.at[s, h, 1, :, hi], r1.at[s, h, 1, :, hi], ring_peer[h](3)))
        return out

    lane = lax.broadcasted_iota(jnp.int32, (CR, 128), 1)

    def masked(s, h):
        if h == 0:
            at = pl.ds(pl.multiple_of(s * SR + x * CR, CR), CR)
            ow, lw = own_n[at, :], low_n[at, :]
        else:
            ats = [pl.ds(pl.multiple_of(s * SR + (4 * j + y) * RS, RS), RS) for j in range(4)]
            ow = jnp.concatenate([own_n[at, :] for at in ats], axis=0)
            lw = jnp.concatenate([low_n[at, :] for at in ats], axis=0)
        pieces = []
        for cc in range(2):
            for m in range(2):
                if h == 0:
                    o0, step = ((2 * m) * 4 + y) * 2 + cc, 8
                else:
                    o0, step = (x * 4 + 2 * m) * 2 + cc, 2
                want = jnp.where(lane < 64, o0, o0 + step).astype(F32)
                pieces.append(jnp.where(ow == want, lw, 0.0).astype(BF16))
        return jnp.concatenate(pieces, axis=1)

    place2 = (y, x)
    peer2 = (y_peer, x_peer)

    def block(h, q):
        return pl.ds(pl.multiple_of(q * RS, RS), RS)

    def collect(s, copies):
        arrived(copies)
        out = []
        for h in range(2):
            lhs = masked(s, h)
            up = (bx, by)[h]
            for n in range(4):
                delta = jnp.dot(
                    lhs, up[:, :, :, cut(n)].reshape(512, TILE), preferred_element_type=F32
                )
                acc[s, h, :, cut(n)] = (acc[s, h, :, cut(n)] + delta) + (
                    r1[s, h, 0, :, cut(n)].astype(F32) + r1[s, h, 1, :, cut(n)].astype(F32)
                )
            t2[s, h] = acc[s, h, block(h, (place2[h] + 2) % 4), :].astype(BF16)
            out.append(go(t2.at[s, h, :, lo], q2.at[s, h, 0], peer2[h](1)))
            out.append(go(t2.at[s, h, :, hi], q2.at[s, h, 1], peer2[h](3)))
        return out

    def near2(s):
        out = []
        for h in range(2):
            t1[s, h, 0, :, QUART:] = acc[s, h, block(h, (place2[h] + 1) % 4), QUART:].astype(BF16)
            out.append(go(t1.at[s, h, 0, :, hi], q1.at[s, h, 0, :, hi], peer2[h](1)))
            t1[s, h, 1, :, :QUART] = acc[s, h, block(h, (place2[h] + 3) % 4), :QUART].astype(BF16)
            out.append(go(t1.at[s, h, 1, :, lo], q1.at[s, h, 1, :, lo], peer2[h](3)))
        return out

    def relay2(s, copies):
        out = []
        for h in range(2):
            arrived(copies[2 * h:2 * h + 2])
            t1[s, h, 0, :, :QUART] = (
                acc[s, h, block(h, (place2[h] + 1) % 4), :QUART] + q2[s, h, 0].astype(F32)
            ).astype(BF16)
            out.append(go(t1.at[s, h, 0, :, lo], q1.at[s, h, 0, :, lo], peer2[h](1)))
            t1[s, h, 1, :, QUART:] = (
                acc[s, h, block(h, (place2[h] + 3) % 4), QUART:] + q2[s, h, 1].astype(F32)
            ).astype(BF16)
            out.append(go(t1.at[s, h, 1, :, hi], q1.at[s, h, 1, :, hi], peer2[h](3)))
        return out

    def finish(s, copies):
        arrived(copies)
        for h in range(2):
            out_ref[s * RS:(s + 1) * RS, h * HALF:(h + 1) * HALF] = (
                acc[s, h, block(h, place2[h]), :]
                + (q1[s, h, 0].astype(F32) + q1[s, h, 1].astype(F32))
            ).astype(BF16)

    for cp in tok_local:
        cp.wait()
    arrived(tok_pre[:2])
    ring(0, 0)
    arrived(tok_pre[2:])
    a_local.wait()
    arrived(a_x)
    a_own = local(a1.at[:, :, a_narrow(y)], a2.at[c, y])
    a_y = [go(a1.at[:, :, a_narrow((y + k) % 4)], a2.at[c, y], y_peer(k)) for k in range(1, 4)]
    ring(0, 1)
    for cp in b_local:
        cp.wait()
    ring(0, 2)
    a_own.wait()
    arrived(a_y)
    a_c = go(a2.at[c], a2.at[c], partner)
    arrived(b_x + b_y)
    b_c = [go(bx.at[c], bx.at[c], partner), go(by.at[c], by.at[c], partner)]
    ring(0, 3)
    ring(1, 0)
    w_local.wait()
    arrived([w_pre, a_c])
    ring_end(0)

    lo0 = low_part(0)
    far0 = far(0)
    ring(1, 1)
    m0 = near(0)
    lo0 = low_x(0, lo0)
    ring(1, 2)
    keep(0)
    m0 += relay(0, far0)
    lo0 = low_y(0, lo0)
    ring(1, 3)
    arrived(b_c)
    low_z(0, lo0)
    ring_end(1)

    lo1 = low_part(1)
    far1 = far(1)
    n0 = collect(0, m0)
    lo1 = low_x(1, lo1)
    m1 = near(1)
    k0 = near2(0)
    keep(1)
    m1 += relay(1, far1)
    lo1 = low_y(1, lo1)
    k0 += relay2(0, n0)
    finish(0, k0)
    low_z(1, lo1)
    n1 = collect(1, m1)
    k1 = near2(1)
    k1 += relay2(1, n1)
    finish(1, k1)
    for cp in sent:
        cp.wait_send()


def body(tokens, query_weight, down, up, request_combination, task_ids, coefficient):
    hbm = pl.BlockSpec(memory_space=pl.ANY)
    vmem = pl.BlockSpec(memory_space=pltpu.VMEM)
    n_sem = 160
    return pl.pallas_call(
        kernel,
        out_shape=jax.ShapeDtypeStruct((64, 2048), BF16),
        in_specs=[hbm, hbm, hbm, hbm, vmem, vmem, vmem],
        out_specs=vmem,
        scratch_shapes=[
            pltpu.VMEM((NS, 16, RS, 1024), BF16),
            pltpu.VMEM((1024, 2048), BF16),
            pltpu.VMEM((4, 8, 4096), BF16),
            pltpu.VMEM((2, 4, 4, 8, 1024), BF16),
            pltpu.VMEM((2, 4, 64, HALF), BF16),
            pltpu.VMEM((2, 4, 64, HALF), BF16),
            pltpu.VMEM((1024, 128), F32),
            pltpu.VMEM((1024, 128), F32),
            pltpu.VMEM((NS, 8, SR), F32),
            pltpu.VMEM((NS, 3, 8, SR), F32),
            pltpu.VMEM((NS, 3, 8, SR), F32),
            pltpu.VMEM((NS, 8, SR), F32),
            pltpu.VMEM((NS, 8, 8, SR), BF16),
            pltpu.VMEM((NS, 2, CR, HALF), BF16),
            pltpu.VMEM((NS, 2, 2, CR, QUART), BF16),
            pltpu.VMEM((NS, 2, 2, CR, HALF), BF16),
            pltpu.VMEM((NS, 2, 2, CR, HALF), BF16),
            pltpu.VMEM((NS, 2, CR, HALF), F32),
            pltpu.VMEM((NS, 2, RS, HALF), BF16),
            pltpu.VMEM((NS, 2, 2, RS, QUART), BF16),
            pltpu.VMEM((NS, 2, 2, RS, HALF), BF16),
            pltpu.VMEM((NS, 2, 2, RS, HALF), BF16),
            pltpu.SemaphoreType.DMA((n_sem,)),
            pltpu.SemaphoreType.DMA((n_sem,)),
            pltpu.SemaphoreType.DMA((16,)),
        ],
        compiler_params=pltpu.CompilerParams(
            collective_id=0, has_side_effects=True, vmem_limit_bytes=67043328
        ),
    )(
        tokens.reshape(2, 2, NS, RS, KC),
        query_weight,
        down.reshape(8, 8, 16384),
        up.reshape(64, 16384),
        request_combination.reshape(1, 2048),
        task_ids.T,
        coefficient.T,
    )


def solution(mesh):
    placed = (
        P("tensor", "adapter"),
        P("adapter", "tensor"),
        P("adapter", None, None),
        P("adapter", None, None),
        P(),
        P(),
        P(),
    )
    return jax.shard_map(
        body, mesh=mesh, in_specs=placed, out_specs=P("adapter", "tensor"), check_vma=False
    )
```

```python
import jax
import jax.numpy as jnp
from jax import lax
from jax.experimental import pallas as pl
from jax.experimental.pallas import tpu as pltpu
from jax.sharding import PartitionSpec as P

NS = 2
RS = 64 // NS
SR = 16 * RS
CR = 4 * RS
KC = 512
HALF = 1024
QUART = 512
TILE = 256
F32 = jnp.float32
BF16 = jnp.bfloat16


def kernel(
    tok_hbm, w_hbm, a_hbm, b_hbm, rows_ref, ids_ref, coef_ref,
    out_ref,
    tok, wf, a1, a2, bx, by,
    own_n, low_n, lt, lx, ly, low_own, low_all,
    s2, r2, s1, r1, acc, t2, q2, t1, q1,
    send_sem, recv_sem, local_sem,
):
    a_idx = lax.axis_index("adapter")
    z = lax.axis_index("tensor")
    x = a_idx // 8
    y = (a_idx // 2) % 4
    c = a_idx % 2
    other = 1 - c

    def dev(xx, yy, cc, zz):
        return {"adapter": (xx * 4 + yy) * 2 + cc, "tensor": zz}

    def x_peer(k):
        return dev((x + k) % 4, y, c, z)

    def y_peer(k):
        return dev(x, (y + k) % 4, c, z)

    def z_peer(k):
        return dev(x, y, c, (z + k) % 8)

    partner = dev(x, y, other, z)
    counter = [0, 0]
    sent = []

    def go(src, dst, device):
        i = counter[0]
        counter[0] += 1
        copy = pltpu.make_async_remote_copy(
            src, dst, send_sem.at[i], recv_sem.at[i],
            device_id=device, device_id_type=pl.DeviceIdType.MESH,
        )
        copy.start()
        sent.append(copy)
        return copy

    def local(src, dst):
        i = counter[1]
        counter[1] += 1
        copy = pltpu.make_async_copy(src, dst, local_sem.at[i])
        copy.start()
        return copy

    def arrived(copies):
        for cp in copies:
            cp.wait_recv()

    my_cols = pl.ds(pl.multiple_of(c * KC, KC), KC)
    tok_local = [
        local(tok_hbm.at[jj, c, s], tok.at[s, 2 * z + jj, :, my_cols])
        for s in range(NS) for jj in range(2)
    ]
    a_wide = lambda xx: pl.ds(pl.multiple_of(xx * 4096, 4096), 4096)
    a_narrow = lambda yy: pl.ds(pl.multiple_of(yy * 1024, 1024), 1024)
    a_local = local(a_hbm.at[z, :, a_wide(x)], a1.at[x])
    b_cols = [pl.ds(pl.multiple_of(z * 2048 + h * HALF, HALF), HALF) for h in range(2)]
    b_local = [
        local(b_hbm.at[:, b_cols[0]], bx.at[c, x]),
        local(b_hbm.at[:, b_cols[1]], by.at[c, y]),
    ]
    w_local = local(w_hbm, wf.at[my_cols, :])

    barrier = pltpu.get_barrier_semaphore()
    peers = [partner]
    peers += [x_peer(k) for k in range(1, 4)] + [y_peer(k) for k in range(1, 4)]
    peers += [z_peer(k) for k in range(1, 8)]
    for peer in peers:
        pl.semaphore_signal(barrier, inc=1, device_id=peer, device_id_type=pl.DeviceIdType.MESH)

    pl.semaphore_wait(barrier, len(peers))

    tok_pre = [
        go(tok_hbm.at[jj, other, s], tok.at[s, 2 * z + jj, :, my_cols], partner)
        for s in range(NS) for jj in range(2)
    ]
    a_x = [go(a_hbm.at[z, :, a_wide((x + k) % 4)], a1.at[x], x_peer(k)) for k in range(1, 4)]
    w_pre = go(w_hbm, wf.at[my_cols, :], partner)

    moving = {}

    def ring(s, k, u):
        ways = ("r", "l") if k < 3 else (("r",), ("l",))[u]
        for way in ways:
            if k > 0:
                moving.pop((s, k - 1, u, way)).wait_recv()
            b = (z - k + 8) % 8 if way == "r" else (z + k) % 8
            src = tok.at[s, 2 * b + u]
            moving[s, k, u, way] = go(src, src, z_peer(1 if way == "r" else 7))

    def ring_end(s):
        for key in [key for key in moving if key[0] == s]:
            moving.pop(key).wait_recv()

    def low_part(s):
        af = a2[...].reshape(256, 1024)
        for k in range(SR // TILE):
            nd = TILE // RS
            part = lax.dot_general(
                af, tok[s, nd * k:nd * (k + 1)].reshape(TILE, 1024),
                (((1,), (1,)), ((), ())), preferred_element_type=F32,
            )
            mine = owner[:, s * SR + TILE * k:s * SR + TILE * (k + 1)]
            total = jnp.zeros((8, TILE), F32)
            for g in range(32):
                o = ((g % 4) * 4 + (g // 4) % 4) * 2 + g // 16
                total += jnp.where(mine == o, part[8 * g:8 * (g + 1)], 0.0)
            lt[s, :, TILE * k:TILE * (k + 1)] = total
        return [go(lt.at[s], lx.at[s, k - 1], x_peer(k)) for k in range(1, 4)]

    def low_x(s, copies):
        arrived(copies)
        low_own[s] = (lt[s] + lx[s, 0]) + (lx[s, 1] + lx[s, 2])
        return [go(low_own.at[s], ly.at[s, k - 1], y_peer(k)) for k in range(1, 4)]

    def low_y(s, copies):
        arrived(copies)
        total = (low_own[s] + ly[s, 0]) + (ly[s, 1] + ly[s, 2])
        low_all[s, z] = (total * weight[:, s * SR:(s + 1) * SR]).astype(BF16)
        return [go(low_all.at[s, z], low_all.at[s, z], z_peer(k)) for k in (4, 3, 5, 2, 6, 1, 7)]

    def low_z(s, copies):
        arrived(copies)
        low_t = low_all[s].astype(F32).reshape(64, SR)
        for k in range(SR // 128):
            tile = low_t[:, 128 * k:128 * (k + 1)]
            low_n[s * SR + 128 * k:s * SR + 128 * (k + 1), :] = jnp.transpose(
                jnp.concatenate([tile, tile], axis=0)
            )

    place = (x, y)
    ring_peer = (x_peer, y_peer)

    def cut(n):
        return slice(n * TILE, (n + 1) * TILE)

    lo, hi = pl.ds(0, QUART), pl.ds(QUART, QUART)

    def dots(s, h, q, first, count, emit):
        if h == 0:
            lhs = tok[s, pl.ds(4 * q, 4)].reshape(CR, 1024)
        else:
            lhs = jnp.concatenate([tok[s, 4 * j + q] for j in range(4)], axis=0)
        for n in range(first, first + count):
            cols = slice(h * HALF + n * TILE, h * HALF + (n + 1) * TILE)
            emit(n, jnp.dot(lhs, wf[:, cols], preferred_element_type=F32))

    def far(s, hs=(0, 1)):
        out = []
        for h in hs:
            def put(n, v, h=h):
                s2[s, h, :, cut(n)] = v.astype(BF16)
            dots(s, h, (place[h] + 2) % 4, 0, 4, put)
            out.append(go(s2.at[s, h, :, lo], r2.at[s, h, 0], ring_peer[h](1)))
            out.append(go(s2.at[s, h, :, hi], r2.at[s, h, 1], ring_peer[h](3)))
        return out

    def near(s, hs=(0, 1)):
        out = []
        for h in hs:
            def put_r(n, v, h=h):
                s1[s, h, 0, :, cut(n)] = v.astype(BF16)
            def put_l(n, v, h=h):
                s1[s, h, 1, :, cut(n)] = v.astype(BF16)
            dots(s, h, (place[h] + 1) % 4, 2, 2, put_r)
            out.append(go(s1.at[s, h, 0, :, hi], r1.at[s, h, 0, :, hi], ring_peer[h](1)))
            dots(s, h, (place[h] + 3) % 4, 0, 2, put_l)
            out.append(go(s1.at[s, h, 1, :, lo], r1.at[s, h, 1, :, lo], ring_peer[h](3)))
        return out

    def keep(s):
        for h in range(2):
            def put(n, v, h=h):
                acc[s, h, :, cut(n)] = v
            dots(s, h, place[h], 0, 4, put)

    def relay(s, copies, hs=(0, 1)):
        out = []
        for h in hs:
            arrived(copies[2 * h:2 * h + 2])
            def add_r(n, v, h=h):
                s1[s, h, 0, :, cut(n)] = (v + r2[s, h, 0, :, cut(n)].astype(F32)).astype(BF16)
            def add_l(n, v, h=h):
                s1[s, h, 1, :, cut(n)] = (v + r2[s, h, 1, :, cut(n - 2)].astype(F32)).astype(BF16)
            dots(s, h, (place[h] + 1) % 4, 0, 2, add_r)
            out.append(go(s1.at[s, h, 0, :, lo], r1.at[s, h, 0, :, lo], ring_peer[h](1)))
            dots(s, h, (place[h] + 3) % 4, 2, 2, add_l)
            out.append(go(s1.at[s, h, 1, :, hi], r1.at[s, h, 1, :, hi], ring_peer[h](3)))
        return out

    lane = lax.broadcasted_iota(jnp.int32, (CR, 128), 1)

    def masked(s, h):
        if h == 0:
            at = pl.ds(pl.multiple_of(s * SR + x * CR, CR), CR)
            ow, lw = own_n[at, :], low_n[at, :]
        else:
            ats = [pl.ds(pl.multiple_of(s * SR + (4 * j + y) * RS, RS), RS) for j in range(4)]
            ow = jnp.concatenate([own_n[at, :] for at in ats], axis=0)
            lw = jnp.concatenate([low_n[at, :] for at in ats], axis=0)
        pieces = []
        for cc in range(2):
            for m in range(2):
                if h == 0:
                    o0, step = ((2 * m) * 4 + y) * 2 + cc, 8
                else:
                    o0, step = (x * 4 + 2 * m) * 2 + cc, 2
                want = jnp.where(lane < 64, o0, o0 + step).astype(F32)
                pieces.append(jnp.where(ow == want, lw, 0.0).astype(BF16))
        return jnp.concatenate(pieces, axis=1)

    place2 = (y, x)
    peer2 = (y_peer, x_peer)

    def block(h, q):
        return pl.ds(pl.multiple_of(q * RS, RS), RS)

    def collect(s, copies):
        arrived(copies)
        out = []
        for h in range(2):
            lhs = masked(s, h)
            up = (bx, by)[h]
            for n in range(4):
                delta = jnp.dot(
                    lhs, up[:, :, :, cut(n)].reshape(512, TILE), preferred_element_type=F32
                )
                acc[s, h, :, cut(n)] = (acc[s, h, :, cut(n)] + delta) + (
                    r1[s, h, 0, :, cut(n)].astype(F32) + r1[s, h, 1, :, cut(n)].astype(F32)
                )
            t2[s, h] = acc[s, h, block(h, (place2[h] + 2) % 4), :].astype(BF16)
            out.append(go(t2.at[s, h, :, lo], q2.at[s, h, 0], peer2[h](1)))
            out.append(go(t2.at[s, h, :, hi], q2.at[s, h, 1], peer2[h](3)))
        return out

    def near2(s):
        out = []
        for h in range(2):
            t1[s, h, 0, :, QUART:] = acc[s, h, block(h, (place2[h] + 1) % 4), QUART:].astype(BF16)
            out.append(go(t1.at[s, h, 0, :, hi], q1.at[s, h, 0, :, hi], peer2[h](1)))
            t1[s, h, 1, :, :QUART] = acc[s, h, block(h, (place2[h] + 3) % 4), :QUART].astype(BF16)
            out.append(go(t1.at[s, h, 1, :, lo], q1.at[s, h, 1, :, lo], peer2[h](3)))
        return out

    def relay2(s, copies):
        out = []
        for h in range(2):
            arrived(copies[2 * h:2 * h + 2])
            t1[s, h, 0, :, :QUART] = (
                acc[s, h, block(h, (place2[h] + 1) % 4), :QUART] + q2[s, h, 0].astype(F32)
            ).astype(BF16)
            out.append(go(t1.at[s, h, 0, :, lo], q1.at[s, h, 0, :, lo], peer2[h](1)))
            t1[s, h, 1, :, QUART:] = (
                acc[s, h, block(h, (place2[h] + 3) % 4), QUART:] + q2[s, h, 1].astype(F32)
            ).astype(BF16)
            out.append(go(t1.at[s, h, 1, :, hi], q1.at[s, h, 1, :, hi], peer2[h](3)))
        return out

    def finish(s, copies):
        arrived(copies)
        for h in range(2):
            out_ref[s * RS:(s + 1) * RS, h * HALF:(h + 1) * HALF] = (
                acc[s, h, block(h, place2[h]), :]
                + (q1[s, h, 0].astype(F32) + q1[s, h, 1].astype(F32))
            ).astype(BF16)

    for cp in tok_local:
        cp.wait()
    arrived(tok_pre[:1])
    ring(0, 0, 0)
    lane8 = lax.broadcasted_iota(jnp.int32, (8, 128), 1)
    per = 128 // RS
    groups = []
    for s in range(NS):
        for g in range(16 // per):
            piece = jnp.zeros((8, 128), jnp.int32)
            for j in range(per):
                d = per * g + j
                raw = jnp.broadcast_to(rows_ref[:, 128 * d:128 * (d + 1)], (8, 128))
                shift = (RS * j - RS * s + 256 - 64 * c) % 128
                piece = jnp.where(lane8 // RS == j, pltpu.roll(raw, shift, 1), piece)
            groups.append(piece[0:1])

    combo = lax.broadcasted_iota(jnp.int32, (4, 512), 1)
    hit = (ids_ref[...] - (combo // 16) * 4) == (z // 2)
    table = 0.25 * jnp.sum(jnp.where(hit, coef_ref[...], 0).astype(F32), axis=0, keepdims=True)
    column = jnp.concatenate(
        [
            jnp.transpose(jnp.broadcast_to(table[:, 128 * k:128 * (k + 1)], (128, 128)))
            for k in range(4)
        ],
        axis=0,
    )
    number = lax.broadcasted_iota(jnp.int32, (512, 128), 0)
    weight = jnp.concatenate(
        [
            jnp.sum(jnp.where(number == g, column, 0.0), axis=0, keepdims=True)
            for g in groups
        ],
        axis=1,
    )
    rows = jnp.concatenate(groups, axis=1)
    owner = rows // 16
    arrived(tok_pre[1:2])
    ring(0, 0, 1)
    owner_f = owner.astype(F32)
    for k in range(8):
        tile = jnp.broadcast_to(owner_f[:, 128 * k:128 * (k + 1)], (128, 128))
        own_n[128 * k:128 * (k + 1), :] = jnp.transpose(tile)

    a_local.wait()
    arrived(tok_pre[2:])
    ring(0, 1, 0)
    ring(0, 1, 1)
    arrived(a_x)
    a_own = local(a1.at[:, :, a_narrow(y)], a2.at[c, y])
    a_y = [go(a1.at[:, :, a_narrow((y + k) % 4)], a2.at[c, y], y_peer(k)) for k in range(1, 4)]
    b_x = [go(b_hbm.at[:, b_cols[0]], bx.at[c, x], x_peer(k)) for k in range(1, 4)]
    b_y = [go(b_hbm.at[:, b_cols[1]], by.at[c, y], y_peer(k)) for k in range(1, 4)]
    ring(0, 2, 0)
    ring(0, 2, 1)
    a_own.wait()
    for cp in b_local:
        cp.wait()
    w_local.wait()
    ring(0, 3, 0)
    ring(1, 0, 0)
    ring(0, 3, 1)
    ring(1, 0, 1)
    arrived(a_y)
    a_c = go(a2.at[c], a2.at[c], partner)
    arrived([w_pre])
    ring_end(0)

    far0 = far(0, (0,))
    ring(1, 1, 0)
    far0 += far(0, (1,))
    ring(1, 1, 1)
    arrived([a_c])
    lo0 = low_part(0)
    m0 = near(0, (0,))
    ring(1, 2, 0)
    m0 += near(0, (1,))
    keep(0)
    ring(1, 2, 1)
    arrived(b_x + b_y)
    b_c = [go(bx.at[c], bx.at[c], partner), go(by.at[c], by.at[c], partner)]
    lo0 = low_x(0, lo0)
    ring(1, 3, 0)
    m0 += relay(0, far0)
    ring(1, 3, 1)
    ring_end(1)

    lo1 = low_part(1)
    far1 = far(1)
    lo0 = low_y(0, lo0)
    m1 = near(1)
    keep(1)
    lo1 = low_x(1, lo1)
    arrived(b_c)
    low_z(0, lo0)
    n0 = collect(0, m0)
    k0 = near2(0)
    lo1 = low_y(1, lo1)
    m1 += relay(1, far1)
    k0 += relay2(0, n0)
    finish(0, k0)
    low_z(1, lo1)
    n1 = collect(1, m1)
    k1 = near2(1)
    k1 += relay2(1, n1)
    finish(1, k1)
    for cp in sent:
        cp.wait_send()


def body(tokens, query_weight, down, up, request_combination, task_ids, coefficient):
    hbm = pl.BlockSpec(memory_space=pl.ANY)
    vmem = pl.BlockSpec(memory_space=pltpu.VMEM)
    n_sem = 160
    return pl.pallas_call(
        kernel,
        out_shape=jax.ShapeDtypeStruct((64, 2048), BF16),
        in_specs=[hbm, hbm, hbm, hbm, vmem, vmem, vmem],
        out_specs=vmem,
        scratch_shapes=[
            pltpu.VMEM((NS, 16, RS, 1024), BF16),
            pltpu.VMEM((1024, 2048), BF16),
            pltpu.VMEM((4, 8, 4096), BF16),
            pltpu.VMEM((2, 4, 4, 8, 1024), BF16),
            pltpu.VMEM((2, 4, 64, HALF), BF16),
            pltpu.VMEM((2, 4, 64, HALF), BF16),
            pltpu.VMEM((1024, 128), F32),
            pltpu.VMEM((1024, 128), F32),
            pltpu.VMEM((NS, 8, SR), F32),
            pltpu.VMEM((NS, 3, 8, SR), F32),
            pltpu.VMEM((NS, 3, 8, SR), F32),
            pltpu.VMEM((NS, 8, SR), F32),
            pltpu.VMEM((NS, 8, 8, SR), BF16),
            pltpu.VMEM((NS, 2, CR, HALF), BF16),
            pltpu.VMEM((NS, 2, 2, CR, QUART), BF16),
            pltpu.VMEM((NS, 2, 2, CR, HALF), BF16),
            pltpu.VMEM((NS, 2, 2, CR, HALF), BF16),
            pltpu.VMEM((NS, 2, CR, HALF), F32),
            pltpu.VMEM((NS, 2, RS, HALF), BF16),
            pltpu.VMEM((NS, 2, 2, RS, QUART), BF16),
            pltpu.VMEM((NS, 2, 2, RS, HALF), BF16),
            pltpu.VMEM((NS, 2, 2, RS, HALF), BF16),
            pltpu.SemaphoreType.DMA((n_sem,)),
            pltpu.SemaphoreType.DMA((n_sem,)),
            pltpu.SemaphoreType.DMA((16,)),
        ],
        compiler_params=pltpu.CompilerParams(
            collective_id=0, has_side_effects=True, vmem_limit_bytes=67043328
        ),
    )(
        tokens.reshape(2, 2, NS, RS, KC),
        query_weight,
        down.reshape(8, 8, 16384),
        up.reshape(64, 16384),
        request_combination.reshape(1, 2048),
        task_ids.T,
        coefficient.T,
    )


def solution(mesh):
    placed = (
        P("tensor", "adapter"),
        P("adapter", "tensor"),
        P("adapter", None, None),
        P("adapter", None, None),
        P(),
        P(),
        P(),
    )
    return jax.shard_map(
        body, mesh=mesh, in_specs=placed, out_specs=P("adapter", "tensor"), check_vma=False
    )
```

```python
import jax
import jax.numpy as jnp
from jax import lax
from jax.experimental import pallas as pl
from jax.experimental.pallas import tpu as pltpu
from jax.sharding import PartitionSpec as P

NS = 4
RS = 64 // NS
SR = 16 * RS
CR = 4 * RS
KC = 512
HALF = 1024
QUART = 512
TILE = 256
F32 = jnp.float32
BF16 = jnp.bfloat16


def kernel(
    tok_hbm, w_hbm, a_hbm, b_hbm, rows_ref, ids_ref, coef_ref,
    out_ref,
    tok, wf, a1, a2, bx, by,
    own_n, low_n, lt, lx, ly, low_own, low_all,
    s2, r2, s1, r1, acc, t1, q1,
    send_sem, recv_sem, local_sem,
):
    a_idx = lax.axis_index("adapter")
    z = lax.axis_index("tensor")
    x = a_idx // 8
    y = (a_idx // 2) % 4
    c = a_idx % 2
    other = 1 - c

    def dev(xx, yy, cc, zz):
        return {"adapter": (xx * 4 + yy) * 2 + cc, "tensor": zz}

    def x_peer(k):
        return dev((x + k) % 4, y, c, z)

    def y_peer(k):
        return dev(x, (y + k) % 4, c, z)

    def z_peer(k):
        return dev(x, y, c, (z + k) % 8)

    partner = dev(x, y, other, z)
    counter = [0, 0]
    sent = []

    def go(src, dst, device):
        i = counter[0]
        counter[0] += 1
        copy = pltpu.make_async_remote_copy(
            src, dst, send_sem.at[i], recv_sem.at[i],
            device_id=device, device_id_type=pl.DeviceIdType.MESH,
        )
        copy.start()
        sent.append(copy)
        return copy

    def local(src, dst):
        i = counter[1]
        counter[1] += 1
        copy = pltpu.make_async_copy(src, dst, local_sem.at[i])
        copy.start()
        return copy

    def arrived(copies):
        for cp in copies:
            cp.wait_recv()

    my_cols = pl.ds(pl.multiple_of(c * KC, KC), KC)
    tok_local = [
        local(tok_hbm.at[jj, c, s], tok.at[s, 2 * z + jj, :, my_cols])
        for s in range(NS) for jj in range(2)
    ]
    a_wide = lambda xx: pl.ds(pl.multiple_of(xx * 4096, 4096), 4096)
    a_narrow = lambda yy: pl.ds(pl.multiple_of(yy * 1024, 1024), 1024)
    a_local = local(a_hbm.at[z, :, a_wide(x)], a1.at[x])
    b_cols = [pl.ds(pl.multiple_of(z * 2048 + h * HALF, HALF), HALF) for h in range(2)]
    b_local = [
        local(b_hbm.at[:, b_cols[0]], bx.at[c, x]),
        local(b_hbm.at[:, b_cols[1]], by.at[c, y]),
    ]
    w_local = local(w_hbm, wf.at[my_cols, :])

    barrier = pltpu.get_barrier_semaphore()
    peers = [partner]
    peers += [x_peer(k) for k in range(1, 4)] + [y_peer(k) for k in range(1, 4)]
    peers += [z_peer(k) for k in range(1, 8)]
    for peer in peers:
        pl.semaphore_signal(barrier, inc=1, device_id=peer, device_id_type=pl.DeviceIdType.MESH)

    pl.semaphore_wait(barrier, len(peers))

    tok_pre = [
        go(tok_hbm.at[jj, other, s], tok.at[s, 2 * z + jj, :, my_cols], partner)
        for s in range(NS) for jj in range(2)
    ]
    a_x = [go(a_hbm.at[z, :, a_wide((x + k) % 4)], a1.at[x], x_peer(k)) for k in range(1, 4)]
    w_pre = go(w_hbm, wf.at[my_cols, :], partner)

    moving = {}

    def ring(s, k, u):
        ways = ("r", "l") if k < 3 else (("r",), ("l",))[u]
        for way in ways:
            if k > 0:
                moving.pop((s, k - 1, u, way)).wait_recv()
            b = (z - k + 8) % 8 if way == "r" else (z + k) % 8
            src = tok.at[s, 2 * b + u]
            moving[s, k, u, way] = go(src, src, z_peer(1 if way == "r" else 7))

    def ring_end(s):
        for key in [key for key in moving if key[0] == s]:
            moving.pop(key).wait_recv()

    def low_part(s):
        af = a2[...].reshape(256, 1024)
        for k in range(SR // TILE):
            nd = TILE // RS
            part = lax.dot_general(
                af, tok[s, nd * k:nd * (k + 1)].reshape(TILE, 1024),
                (((1,), (1,)), ((), ())), preferred_element_type=F32,
            )
            mine = owner[:, s * SR + TILE * k:s * SR + TILE * (k + 1)]
            total = jnp.zeros((8, TILE), F32)
            for g in range(32):
                o = ((g % 4) * 4 + (g // 4) % 4) * 2 + g // 16
                total += jnp.where(mine == o, part[8 * g:8 * (g + 1)], 0.0)
            lt[s, :, TILE * k:TILE * (k + 1)] = total
        return [go(lt.at[s], lx.at[s, k - 1], x_peer(k)) for k in range(1, 4)]

    def low_x(s, copies):
        arrived(copies)
        low_own[s] = (lt[s] + lx[s, 0]) + (lx[s, 1] + lx[s, 2])
        return [go(low_own.at[s], ly.at[s, k - 1], y_peer(k)) for k in range(1, 4)]

    def low_y(s, copies):
        arrived(copies)
        total = (low_own[s] + ly[s, 0]) + (ly[s, 1] + ly[s, 2])
        low_all[s, z] = (total * weight[:, s * SR:(s + 1) * SR]).astype(BF16)
        return [go(low_all.at[s, z], low_all.at[s, z], z_peer(k)) for k in (4, 3, 5, 2, 6, 1, 7)]

    def low_z(s, copies):
        arrived(copies)
        low_t = low_all[s].astype(F32).reshape(64, SR)
        for k in range(SR // 128):
            tile = low_t[:, 128 * k:128 * (k + 1)]
            low_n[s * SR + 128 * k:s * SR + 128 * (k + 1), :] = jnp.transpose(
                jnp.concatenate([tile, tile], axis=0)
            )

    place = (x, y)
    ring_peer = (x_peer, y_peer)

    def cut(n):
        return slice(n * TILE, (n + 1) * TILE)

    lo, hi = pl.ds(0, QUART), pl.ds(QUART, QUART)

    def dots(s, h, q, first, count, emit):
        if h == 0:
            lhs = tok[s, pl.ds(4 * q, 4)].reshape(CR, 1024)
        else:
            lhs = jnp.concatenate([tok[s, 4 * j + q] for j in range(4)], axis=0)
        for n in range(first, first + count):
            cols = slice(h * HALF + n * TILE, h * HALF + (n + 1) * TILE)
            emit(n, jnp.dot(lhs, wf[:, cols], preferred_element_type=F32))

    def far(s, hs=(0, 1)):
        out = []
        for h in hs:
            def put(n, v, h=h):
                s2[s, h, :, cut(n)] = v.astype(BF16)
            dots(s, h, (place[h] + 2) % 4, 0, 4, put)
            out.append(go(s2.at[s, h, :, lo], r2.at[s, h, 0], ring_peer[h](1)))
            out.append(go(s2.at[s, h, :, hi], r2.at[s, h, 1], ring_peer[h](3)))
        return out

    def near(s, hs=(0, 1)):
        out = []
        for h in hs:
            def put_r(n, v, h=h):
                s1[s, h, 0, :, cut(n)] = v.astype(BF16)
            def put_l(n, v, h=h):
                s1[s, h, 1, :, cut(n)] = v.astype(BF16)
            dots(s, h, (place[h] + 1) % 4, 2, 2, put_r)
            out.append(go(s1.at[s, h, 0, :, hi], r1.at[s, h, 0, :, hi], ring_peer[h](1)))
            dots(s, h, (place[h] + 3) % 4, 0, 2, put_l)
            out.append(go(s1.at[s, h, 1, :, lo], r1.at[s, h, 1, :, lo], ring_peer[h](3)))
        return out

    def keep(s, hs=(0, 1)):
        for h in hs:
            def put(n, v, h=h):
                acc[s, h, :, cut(n)] = v
            dots(s, h, place[h], 0, 4, put)

    def relay(s, copies, hs=(0, 1)):
        out = []
        for h in hs:
            arrived(copies)
            def add_r(n, v, h=h):
                s1[s, h, 0, :, cut(n)] = (v + r2[s, h, 0, :, cut(n)].astype(F32)).astype(BF16)
            def add_l(n, v, h=h):
                s1[s, h, 1, :, cut(n)] = (v + r2[s, h, 1, :, cut(n - 2)].astype(F32)).astype(BF16)
            dots(s, h, (place[h] + 1) % 4, 0, 2, add_r)
            out.append(go(s1.at[s, h, 0, :, lo], r1.at[s, h, 0, :, lo], ring_peer[h](1)))
            dots(s, h, (place[h] + 3) % 4, 2, 2, add_l)
            out.append(go(s1.at[s, h, 1, :, hi], r1.at[s, h, 1, :, hi], ring_peer[h](3)))
        return out

    lane = lax.broadcasted_iota(jnp.int32, (CR, 128), 1)

    def masked(s, h):
        if h == 0:
            at = pl.ds(pl.multiple_of(s * SR + x * CR, CR), CR)
            ow, lw = own_n[at, :], low_n[at, :]
        else:
            ats = [pl.ds(pl.multiple_of(s * SR + (4 * j + y) * RS, RS), RS) for j in range(4)]
            ow = jnp.concatenate([own_n[at, :] for at in ats], axis=0)
            lw = jnp.concatenate([low_n[at, :] for at in ats], axis=0)
        pieces = []
        for cc in range(2):
            for m in range(2):
                if h == 0:
                    o0, step = ((2 * m) * 4 + y) * 2 + cc, 8
                else:
                    o0, step = (x * 4 + 2 * m) * 2 + cc, 2
                want = jnp.where(lane < 64, o0, o0 + step).astype(F32)
                pieces.append(jnp.where(ow == want, lw, 0.0).astype(BF16))
        return jnp.concatenate(pieces, axis=1)

    place2 = (y, x)
    peer2 = (y_peer, x_peer)

    def block(h, q):
        return pl.ds(pl.multiple_of(q * RS, RS), RS)

    def collect(s, h, copies):
        arrived(copies)
        lhs = masked(s, h)
        up = (bx, by)[h]
        for n in range(4):
            delta = jnp.dot(
                lhs, up[:, :, :, cut(n)].reshape(512, TILE), preferred_element_type=F32
            )
            acc[s, h, :, cut(n)] = (acc[s, h, :, cut(n)] + delta) + (
                r1[s, h, 0, :, cut(n)].astype(F32) + r1[s, h, 1, :, cut(n)].astype(F32)
            )
        out = []
        for k in (2, 1, 3):
            t1[s, h, k - 1] = acc[s, h, block(h, (place2[h] + k) % 4), :].astype(BF16)
            out.append(go(t1.at[s, h, k - 1], q1.at[s, h, k - 1], peer2[h](k)))
        return out

    def finish(s, h, copies):
        arrived(copies)
        out_ref[s * RS:(s + 1) * RS, h * HALF:(h + 1) * HALF] = (
            (acc[s, h, block(h, place2[h]), :] + q1[s, h, 0].astype(F32))
            + (q1[s, h, 1].astype(F32) + q1[s, h, 2].astype(F32))
        ).astype(BF16)

    lows, fars, mids, ends = {}, {}, {}, {}
    for cp in tok_local:
        cp.wait()
    arrived(tok_pre[0:1])
    ring(0, 0, 0)
    lane8 = lax.broadcasted_iota(jnp.int32, (8, 128), 1)
    per = 128 // RS
    groups = []
    for s in range(NS):
        for g in range(16 // per):
            piece = jnp.zeros((8, 128), jnp.int32)
            for j in range(per):
                d = per * g + j
                raw = jnp.broadcast_to(rows_ref[:, 128 * d:128 * (d + 1)], (8, 128))
                shift = (RS * j - RS * s + 256 - 64 * c) % 128
                piece = jnp.where(lane8 // RS == j, pltpu.roll(raw, shift, 1), piece)
            groups.append(piece[0:1])

    combo = lax.broadcasted_iota(jnp.int32, (4, 512), 1)
    hit = (ids_ref[...] - (combo // 16) * 4) == (z // 2)
    table = 0.25 * jnp.sum(jnp.where(hit, coef_ref[...], 0).astype(F32), axis=0, keepdims=True)
    column = jnp.concatenate(
        [
            jnp.transpose(jnp.broadcast_to(table[:, 128 * k:128 * (k + 1)], (128, 128)))
            for k in range(4)
        ],
        axis=0,
    )
    number = lax.broadcasted_iota(jnp.int32, (512, 128), 0)
    weight = jnp.concatenate(
        [
            jnp.sum(jnp.where(number == g, column, 0.0), axis=0, keepdims=True)
            for g in groups
        ],
        axis=1,
    )
    rows = jnp.concatenate(groups, axis=1)
    owner = rows // 16
    arrived(tok_pre[1:2])
    ring(0, 0, 1)
    arrived(tok_pre[2:3])
    ring(1, 0, 0)
    arrived(tok_pre[3:4])
    ring(1, 0, 1)
    owner_f = owner.astype(F32)
    for k in range(8):
        tile = jnp.broadcast_to(owner_f[:, 128 * k:128 * (k + 1)], (128, 128))
        own_n[128 * k:128 * (k + 1), :] = jnp.transpose(tile)

    ring(0, 1, 0)
    ring(0, 1, 1)
    a_local.wait()
    arrived(a_x)
    a_own = local(a1.at[:, :, a_narrow(y)], a2.at[c, y])
    a_y = [go(a1.at[:, :, a_narrow((y + k) % 4)], a2.at[c, y], y_peer(k)) for k in range(1, 4)]
    b_x = [go(b_hbm.at[:, b_cols[0]], bx.at[c, x], x_peer(k)) for k in range(1, 4)]
    b_y = [go(b_hbm.at[:, b_cols[1]], by.at[c, y], y_peer(k)) for k in range(1, 4)]
    ring(1, 1, 0)
    ring(1, 1, 1)
    ring(0, 2, 0)
    arrived(tok_pre[4:5])
    ring(2, 0, 0)
    ring(0, 2, 1)
    arrived(tok_pre[5:6])
    ring(2, 0, 1)
    ring(1, 2, 0)
    arrived(tok_pre[6:7])
    ring(3, 0, 0)
    ring(1, 2, 1)
    arrived(tok_pre[7:8])
    ring(3, 0, 1)
    ring(0, 3, 0)
    ring(2, 1, 0)
    a_own.wait()
    arrived(a_y)
    a_c = go(a2.at[c], a2.at[c], partner)
    ring(0, 3, 1)
    ring(2, 1, 1)
    ring(1, 3, 0)
    ring(3, 1, 0)
    ring(1, 3, 1)
    ring(3, 1, 1)
    ring(2, 2, 0)
    arrived([a_c])
    ring_end(0)
    lows[0] = low_part(0)
    w_local.wait()
    arrived([w_pre])
    fars[0, 1] = far(0, (1,))
    fars[0, 0] = far(0, (0,))
    mids[0, 1] = near(0, (1,))
    ring(2, 2, 1)
    mids[0, 0] = near(0, (0,))
    for cp in b_local:
        cp.wait()
    arrived(b_x + b_y)
    b_c = [go(bx.at[c], bx.at[c], partner), go(by.at[c], by.at[c], partner)]
    keep(0, (0,))
    keep(0, (1,))
    ring(3, 2, 0)
    ring_end(1)
    lows[1] = low_part(1)
    fars[1, 1] = far(1, (1,))
    fars[1, 0] = far(1, (0,))
    mids[1, 0] = near(1, (0,))
    ring(3, 2, 1)
    mids[1, 1] = near(1, (1,))
    keep(1, (1,))
    keep(1, (0,))
    ring(2, 3, 0)
    lows[0] = low_x(0, lows[0])
    ring(2, 3, 1)
    mids[0, 1] += relay(0, fars[0, 1], (1,))
    mids[0, 0] += relay(0, fars[0, 0], (0,))
    ring(3, 3, 0)
    ring(3, 3, 1)
    lows[1] = low_x(1, lows[1])
    ring_end(2)
    lows[2] = low_part(2)
    mids[1, 1] += relay(1, fars[1, 1], (1,))
    mids[1, 0] += relay(1, fars[1, 0], (0,))
    fars[2, 0] = far(2, (0,))
    fars[2, 1] = far(2, (1,))
    mids[2, 0] = near(2, (0,))
    mids[2, 1] = near(2, (1,))
    keep(2, (1,))
    keep(2, (0,))
    ring_end(3)
    lows[3] = low_part(3)
    fars[3, 1] = far(3, (1,))
    fars[3, 0] = far(3, (0,))
    mids[3, 0] = near(3, (0,))
    lows[0] = low_y(0, lows[0])
    mids[3, 1] = near(3, (1,))
    keep(3, (0,))
    keep(3, (1,))
    lows[1] = low_y(1, lows[1])
    lows[2] = low_x(2, lows[2])
    mids[2, 1] += relay(2, fars[2, 1], (1,))
    mids[2, 0] += relay(2, fars[2, 0], (0,))
    low_z(0, lows[0])
    arrived(b_c)
    ends[0, 0] = collect(0, 0, mids[0, 0])
    lows[3] = low_x(3, lows[3])
    ends[0, 1] = collect(0, 1, mids[0, 1])
    mids[3, 0] += relay(3, fars[3, 0], (0,))
    mids[3, 1] += relay(3, fars[3, 1], (1,))
    low_z(1, lows[1])
    ends[1, 1] = collect(1, 1, mids[1, 1])
    ends[1, 0] = collect(1, 0, mids[1, 0])
    lows[2] = low_y(2, lows[2])
    finish(0, 0, ends[0, 0])
    finish(0, 1, ends[0, 1])
    lows[3] = low_y(3, lows[3])
    low_z(2, lows[2])
    ends[2, 1] = collect(2, 1, mids[2, 1])
    ends[2, 0] = collect(2, 0, mids[2, 0])
    finish(1, 0, ends[1, 0])
    finish(1, 1, ends[1, 1])
    low_z(3, lows[3])
    ends[3, 1] = collect(3, 1, mids[3, 1])
    ends[3, 0] = collect(3, 0, mids[3, 0])
    finish(2, 1, ends[2, 1])
    finish(2, 0, ends[2, 0])
    finish(3, 1, ends[3, 1])
    finish(3, 0, ends[3, 0])
    for cp in sent:
        cp.wait_send()


def body(tokens, query_weight, down, up, request_combination, task_ids, coefficient):
    hbm = pl.BlockSpec(memory_space=pl.ANY)
    vmem = pl.BlockSpec(memory_space=pltpu.VMEM)
    n_sem = 256
    return pl.pallas_call(
        kernel,
        out_shape=jax.ShapeDtypeStruct((64, 2048), BF16),
        in_specs=[hbm, hbm, hbm, hbm, vmem, vmem, vmem],
        out_specs=vmem,
        scratch_shapes=[
            pltpu.VMEM((NS, 16, RS, 1024), BF16),
            pltpu.VMEM((1024, 2048), BF16),
            pltpu.VMEM((4, 8, 4096), BF16),
            pltpu.VMEM((2, 4, 4, 8, 1024), BF16),
            pltpu.VMEM((2, 4, 64, HALF), BF16),
            pltpu.VMEM((2, 4, 64, HALF), BF16),
            pltpu.VMEM((1024, 128), F32),
            pltpu.VMEM((1024, 128), F32),
            pltpu.VMEM((NS, 8, SR), F32),
            pltpu.VMEM((NS, 3, 8, SR), F32),
            pltpu.VMEM((NS, 3, 8, SR), F32),
            pltpu.VMEM((NS, 8, SR), F32),
            pltpu.VMEM((NS, 8, 8, SR), BF16),
            pltpu.VMEM((NS, 2, CR, HALF), BF16),
            pltpu.VMEM((NS, 2, 2, CR, QUART), BF16),
            pltpu.VMEM((NS, 2, 2, CR, HALF), BF16),
            pltpu.VMEM((NS, 2, 2, CR, HALF), BF16),
            pltpu.VMEM((NS, 2, CR, HALF), F32),
            pltpu.VMEM((NS, 2, 3, RS, HALF), BF16),
            pltpu.VMEM((NS, 2, 3, RS, HALF), BF16),
            pltpu.SemaphoreType.DMA((n_sem,)),
            pltpu.SemaphoreType.DMA((n_sem,)),
            pltpu.SemaphoreType.DMA((16,)),
        ],
        compiler_params=pltpu.CompilerParams(
            collective_id=0, has_side_effects=True, vmem_limit_bytes=67043328
        ),
    )(
        tokens.reshape(2, 2, NS, RS, KC),
        query_weight,
        down.reshape(8, 8, 16384),
        up.reshape(64, 16384),
        request_combination.reshape(1, 2048),
        task_ids.T,
        coefficient.T,
    )


def solution(mesh):
    placed = (
        P("tensor", "adapter"),
        P("adapter", "tensor"),
        P("adapter", None, None),
        P("adapter", None, None),
        P(),
        P(),
        P(),
    )
    return jax.shard_map(
        body, mesh=mesh, in_specs=placed, out_specs=P("adapter", "tensor"), check_vma=False
    )
```

```python
import math

import jax
import jax.numpy as jnp
from jax import lax
from jax.experimental import pallas as pl
from jax.experimental.pallas import tpu as pltpu
from jax.sharding import PartitionSpec as P

NS = 4
RS = 64 // NS
SR = 16 * RS
CR = 4 * RS
KC = 512
HALF = 1024
QUART = 512
TILE = 256
F32 = jnp.float32
BF16 = jnp.bfloat16


def kernel(
    tok_hbm, w_hbm, a_hbm, b_hbm, rows_ref, ids_ref, coef_ref,
    out_ref,
    tok, wf, a1, a2, bx, by,
    own_n, low_n, lt, lx, ly, low_own, low_all,
    s2, r2, s1, r1, acc, t1, q1,
    send_sem, recv_sem, local_sem,
):
    a_idx = lax.axis_index("adapter")
    z = lax.axis_index("tensor")
    x = a_idx // 8
    y = (a_idx // 2) % 4
    c = a_idx % 2
    other = 1 - c

    def dev(xx, yy, cc, zz):
        return {"adapter": (xx * 4 + yy) * 2 + cc, "tensor": zz}

    def x_peer(k):
        return dev((x + k) % 4, y, c, z)

    def y_peer(k):
        return dev(x, (y + k) % 4, c, z)

    def z_peer(k):
        return dev(x, y, c, (z + k) % 8)

    partner = dev(x, y, other, z)
    counter = [0, 0]
    sent = [0] * 5
    START, UP, RING, SUMS, LOWS = range(5)

    def arrival():
        counter[0] += 1
        return counter[0] - 1

    def go(src, dst, device, mark, group):
        pltpu.make_async_remote_copy(
            src, dst, send_sem.at[group], recv_sem.at[mark],
            device_id=device, device_id_type=pl.DeviceIdType.MESH,
        ).start()
        sent[group] += math.prod(src.shape) * src.dtype.itemsize

    def arrived(mark, ref):
        pltpu.make_async_remote_copy(
            ref, ref, send_sem.at[0], recv_sem.at[mark],
            device_id=partner, device_id_type=pl.DeviceIdType.MESH,
        ).wait_recv()

    def gone(group, ref):
        row = math.prod(ref.shape[1:]) * ref.dtype.itemsize
        part = ref.at[pl.ds(0, sent[group] // row)]
        pltpu.make_async_remote_copy(
            part, part, send_sem.at[group], recv_sem.at[0],
            device_id=partner, device_id_type=pl.DeviceIdType.MESH,
        ).wait_send()

    def local(src, dst):
        i = counter[1]
        counter[1] += 1
        copy = pltpu.make_async_copy(src, dst, local_sem.at[i])
        copy.start()
        return copy

    my_cols = pl.ds(pl.multiple_of(c * KC, KC), KC)
    tok_local = [
        local(tok_hbm.at[:, c, s], tok.at[s, c, pl.ds(2 * z, 2)]) for s in range(NS)
    ]
    a_wide = lambda xx: pl.ds(pl.multiple_of(xx * 4096, 4096), 4096)
    a_narrow = lambda yy: pl.ds(pl.multiple_of(yy * 1024, 1024), 1024)
    a_local = local(a_hbm.at[z, :, a_wide(x)], a1.at[x])
    b_cols = [pl.ds(pl.multiple_of(z * 2048 + h * HALF, HALF), HALF) for h in range(2)]
    b_local = [
        local(b_hbm.at[:, b_cols[0]], bx.at[c, x]),
        local(b_hbm.at[:, b_cols[1]], by.at[c, y]),
    ]
    w_local = local(w_hbm, wf.at[my_cols, :])

    barrier = pltpu.get_barrier_semaphore()
    peers = [partner]
    peers += [x_peer(k) for k in range(1, 4)] + [y_peer(k) for k in range(1, 4)]
    peers += [z_peer(k) for k in range(1, 8)]
    for peer in peers:
        pl.semaphore_signal(barrier, inc=1, device_id=peer, device_id_type=pl.DeviceIdType.MESH)

    pl.semaphore_wait(barrier, len(peers))

    tok_pre = [arrival() for _ in range(NS)]

    def exchange(s):
        go(tok_hbm.at[:, other, s], tok.at[s, c, pl.ds(2 * z, 2)], partner, tok_pre[s], START)

    a_x, w_pre, a_y, a_c, b_x, b_y, b_c = [arrival() for _ in range(7)]

    moving = {}

    def ring(s, k, u):
        half = c if u == 0 else other
        if k > 0:
            arrived(moving.pop((s, k - 1, u)), tok.at[s, 0, pl.ds(0, 4)])
        moving[s, k, u] = mark = arrival()
        if k < 3 or u == 0:
            src = tok.at[s, half, pl.ds(2 * ((z - k + 8) % 8), 2)]
            go(src, src, z_peer(1), mark, RING)
        if k < 3 or u == 1:
            src = tok.at[s, half, pl.ds(2 * ((z + k) % 8), 2)]
            go(src, src, z_peer(7), mark, RING)

    def ring_end(s):
        for u in range(2):
            arrived(moving.pop((s, 3, u)), tok.at[s, 0, pl.ds(0, 2)])

    def wide(halves):
        return jnp.concatenate(halves, axis=1)

    def low_part(s):
        af = a2[...].reshape(256, 1024)
        for k in range(SR // TILE):
            nd = TILE // RS
            part = lax.dot_general(
                af, wide([tok[s, kc, nd * k:nd * (k + 1)].reshape(TILE, KC) for kc in range(2)]),
                (((1,), (1,)), ((), ())), preferred_element_type=F32,
            )
            mine = owner[:, s * SR + TILE * k:s * SR + TILE * (k + 1)]
            total = jnp.zeros((8, TILE), F32)
            for g in range(32):
                o = ((g % 4) * 4 + (g // 4) % 4) * 2 + g // 16
                total += jnp.where(mine == o, part[8 * g:8 * (g + 1)], 0.0)
            lt[s, :, TILE * k:TILE * (k + 1)] = total
        mark = arrival()
        for k in range(1, 4):
            go(lt.at[s], lx.at[s, k - 1], x_peer(k), mark, LOWS)
        return mark

    def low_x(s, mark):
        arrived(mark, lx.at[s])
        low_own[s] = (lt[s] + lx[s, 0]) + (lx[s, 1] + lx[s, 2])
        mark = arrival()
        for k in range(1, 4):
            go(low_own.at[s], ly.at[s, k - 1], y_peer(k), mark, LOWS)
        return mark

    def low_y(s, mark):
        arrived(mark, ly.at[s])
        total = (low_own[s] + ly[s, 0]) + (ly[s, 1] + ly[s, 2])
        low_all[s, z] = (total * weight[:, s * SR:(s + 1) * SR]).astype(BF16)
        mark = arrival()
        for k in (4, 3, 5, 2, 6, 1, 7):
            go(low_all.at[s, z], low_all.at[s, z], z_peer(k), mark, LOWS)
        return mark

    def low_z(s, mark):
        arrived(mark, low_all.at[s, pl.ds(0, 7)])
        low_t = low_all[s].astype(F32).reshape(64, SR)
        for k in range(SR // 128):
            tile = low_t[:, 128 * k:128 * (k + 1)]
            low_n[s * SR + 128 * k:s * SR + 128 * (k + 1), :] = jnp.transpose(
                jnp.concatenate([tile, tile], axis=0)
            )

    place = (x, y)
    ring_peer = (x_peer, y_peer)

    def cut(n):
        return slice(n * TILE, (n + 1) * TILE)

    lo, hi = pl.ds(0, QUART), pl.ds(QUART, QUART)

    def dots(s, h, q, first, count, emit):
        if h == 0:
            lhs = wide([tok[s, kc, pl.ds(4 * q, 4)].reshape(CR, KC) for kc in range(2)])
        else:
            lhs = wide([
                jnp.concatenate([tok[s, kc, 4 * j + q] for j in range(4)], axis=0)
                for kc in range(2)
            ])
        for n in range(first, first + count):
            cols = slice(h * HALF + n * TILE, h * HALF + (n + 1) * TILE)
            emit(n, jnp.dot(lhs, wf[:, cols], preferred_element_type=F32))

    def far(s, h):
        def put(n, v):
            s2[s, h, :, cut(n)] = v.astype(BF16)
        dots(s, h, (place[h] + 2) % 4, 0, 4, put)
        mark = arrival()
        go(s2.at[s, h, :, lo], r2.at[s, h, 0], ring_peer[h](1), mark, SUMS)
        go(s2.at[s, h, :, hi], r2.at[s, h, 1], ring_peer[h](3), mark, SUMS)
        return mark

    def near(s, h):
        def put_r(n, v):
            s1[s, h, 0, :, cut(n)] = v.astype(BF16)
        def put_l(n, v):
            s1[s, h, 1, :, cut(n)] = v.astype(BF16)
        mark = arrival()
        dots(s, h, (place[h] + 1) % 4, 2, 2, put_r)
        go(s1.at[s, h, 0, :, hi], r1.at[s, h, 0, :, hi], ring_peer[h](1), mark, SUMS)
        dots(s, h, (place[h] + 3) % 4, 0, 2, put_l)
        go(s1.at[s, h, 1, :, lo], r1.at[s, h, 1, :, lo], ring_peer[h](3), mark, SUMS)
        return mark

    def keep(s, h):
        def put(n, v):
            acc[s, h, :, cut(n)] = v
        dots(s, h, place[h], 0, 4, put)

    def relay(s, h, ready, mark):
        arrived(ready, r2.at[s, h])
        def add_r(n, v):
            s1[s, h, 0, :, cut(n)] = (v + r2[s, h, 0, :, cut(n)].astype(F32)).astype(BF16)
        def add_l(n, v):
            s1[s, h, 1, :, cut(n)] = (v + r2[s, h, 1, :, cut(n - 2)].astype(F32)).astype(BF16)
        dots(s, h, (place[h] + 1) % 4, 0, 2, add_r)
        go(s1.at[s, h, 0, :, lo], r1.at[s, h, 0, :, lo], ring_peer[h](1), mark, SUMS)
        dots(s, h, (place[h] + 3) % 4, 2, 2, add_l)
        go(s1.at[s, h, 1, :, hi], r1.at[s, h, 1, :, hi], ring_peer[h](3), mark, SUMS)

    lane = lax.broadcasted_iota(jnp.int32, (CR, 128), 1)

    def masked(s, h):
        if h == 0:
            at = pl.ds(pl.multiple_of(s * SR + x * CR, CR), CR)
            ow, lw = own_n[at, :], low_n[at, :]
        else:
            ats = [pl.ds(pl.multiple_of(s * SR + (4 * j + y) * RS, RS), RS) for j in range(4)]
            ow = jnp.concatenate([own_n[at, :] for at in ats], axis=0)
            lw = jnp.concatenate([low_n[at, :] for at in ats], axis=0)
        pieces = []
        for cc in range(2):
            for m in range(2):
                if h == 0:
                    o0, step = ((2 * m) * 4 + y) * 2 + cc, 8
                else:
                    o0, step = (x * 4 + 2 * m) * 2 + cc, 2
                want = jnp.where(lane < 64, o0, o0 + step).astype(F32)
                pieces.append(jnp.where(ow == want, lw, 0.0).astype(BF16))
        return jnp.concatenate(pieces, axis=1)

    place2 = (y, x)
    peer2 = (y_peer, x_peer)

    def block(h, q):
        return pl.ds(pl.multiple_of(q * RS, RS), RS)

    def collect(s, h, mark):
        arrived(mark, r1.at[s, h])
        lhs = masked(s, h)
        up = (bx, by)[h]
        for n in range(4):
            delta = jnp.dot(
                lhs, up[:, :, :, cut(n)].reshape(512, TILE), preferred_element_type=F32
            )
            acc[s, h, :, cut(n)] = (acc[s, h, :, cut(n)] + delta) + (
                r1[s, h, 0, :, cut(n)].astype(F32) + r1[s, h, 1, :, cut(n)].astype(F32)
            )
        mark = arrival()
        for k in (2, 1, 3):
            t1[s, h, k - 1] = acc[s, h, block(h, (place2[h] + k) % 4), :].astype(BF16)
            go(t1.at[s, h, k - 1], q1.at[s, h, k - 1], peer2[h](k), mark, SUMS)
        return mark

    def finish(s, h, mark):
        arrived(mark, q1.at[s, h])
        out_ref[s * RS:(s + 1) * RS, h * HALF:(h + 1) * HALF] = (
            (acc[s, h, block(h, place2[h]), :] + q1[s, h, 0].astype(F32))
            + (q1[s, h, 1].astype(F32) + q1[s, h, 2].astype(F32))
        ).astype(BF16)

    lows, fars, mids, ends = {}, {}, {}, {}
    for cp in tok_local:
        cp.wait()
    ring(0, 0, 0)
    for s in range(NS):
        exchange(s)
    for k in range(1, 4):
        go(a_hbm.at[z, :, a_wide((x + k) % 4)], a1.at[x], x_peer(k), a_x, START)
    go(w_hbm, wf.at[my_cols, :], partner, w_pre, START)
    ring(1, 0, 0)
    lane8 = lax.broadcasted_iota(jnp.int32, (8, 128), 1)
    per = 128 // RS
    groups = []
    for s in range(NS):
        for g in range(16 // per):
            piece = jnp.zeros((8, 128), jnp.int32)
            for j in range(per):
                d = per * g + j
                raw = jnp.broadcast_to(rows_ref[:, 128 * d:128 * (d + 1)], (8, 128))
                shift = (RS * j - RS * s + 256 - 64 * c) % 128
                piece = jnp.where(lane8 // RS == j, pltpu.roll(raw, shift, 1), piece)
            groups.append(piece[0:1])

    combo = lax.broadcasted_iota(jnp.int32, (4, 512), 1)
    hit = (ids_ref[...] - (combo // 16) * 4) == (z // 2)
    table = 0.25 * jnp.sum(jnp.where(hit, coef_ref[...], 0).astype(F32), axis=0, keepdims=True)
    column = jnp.concatenate(
        [
            jnp.transpose(jnp.broadcast_to(table[:, 128 * k:128 * (k + 1)], (128, 128)))
            for k in range(4)
        ],
        axis=0,
    )
    number = lax.broadcasted_iota(jnp.int32, (512, 128), 0)
    weight = jnp.concatenate(
        [
            jnp.sum(jnp.where(number == g, column, 0.0), axis=0, keepdims=True)
            for g in groups
        ],
        axis=1,
    )
    rows = jnp.concatenate(groups, axis=1)
    owner = rows // 16
    arrived(tok_pre[0], tok.at[0, 0, pl.ds(0, 2)])
    ring(0, 0, 1)
    owner_f = owner.astype(F32)
    for k in range(8):
        tile = jnp.broadcast_to(owner_f[:, 128 * k:128 * (k + 1)], (128, 128))
        own_n[128 * k:128 * (k + 1), :] = jnp.transpose(tile)

    arrived(tok_pre[1], tok.at[1, 0, pl.ds(0, 2)])
    ring(1, 0, 1)
    ring(0, 1, 0)
    ring(1, 1, 0)
    ring(0, 1, 1)
    ring(1, 1, 1)
    a_local.wait()
    arrived(a_x, a1.at[pl.ds(0, 3)])
    a_own = local(a1.at[:, :, a_narrow(y)], a2.at[c, y])
    for k in range(1, 4):
        go(a1.at[:, :, a_narrow((y + k) % 4)], a2.at[c, y], y_peer(k), a_y, START)
    for k in range(1, 4):
        go(b_hbm.at[:, b_cols[0]], bx.at[c, x], x_peer(k), b_x, UP)
        go(b_hbm.at[:, b_cols[1]], by.at[c, y], y_peer(k), b_y, UP)
    ring(0, 2, 0)
    ring(2, 0, 0)
    ring(1, 2, 0)
    ring(3, 0, 0)
    ring(0, 2, 1)
    arrived(tok_pre[2], tok.at[2, 0, pl.ds(0, 2)])
    ring(2, 0, 1)
    ring(1, 2, 1)
    arrived(tok_pre[3], tok.at[3, 0, pl.ds(0, 2)])
    ring(3, 0, 1)
    ring(0, 3, 0)
    ring(2, 1, 0)
    ring(1, 3, 0)
    ring(3, 1, 0)
    a_own.wait()
    arrived(a_y, a2.at[0, pl.ds(0, 3)])
    go(a2.at[c], a2.at[c], partner, a_c, START)
    ring(0, 3, 1)
    ring(2, 1, 1)
    ring(1, 3, 1)
    ring(3, 1, 1)
    ring(2, 2, 0)
    ring(3, 2, 0)
    arrived(a_c, a2.at[0])
    ring_end(0)
    lows[0] = low_part(0)
    w_local.wait()
    arrived(w_pre, wf.at[pl.ds(0, KC)])
    fars[0, 0] = far(0, 0)
    fars[0, 1] = far(0, 1)
    mids[0, 0] = near(0, 0)
    ring(2, 2, 1)
    mids[0, 1] = near(0, 1)
    for cp in b_local:
        cp.wait()
    arrived(b_x, bx.at[0, pl.ds(0, 3)])
    arrived(b_y, by.at[0, pl.ds(0, 3)])
    for ref in (bx, by):
        go(ref.at[c], ref.at[c], partner, b_c, UP)
    keep(0, 0)
    ring_end(1)
    lows[1] = low_part(1)
    fars[1, 1] = far(1, 1)
    fars[1, 0] = far(1, 0)
    mids[1, 1] = near(1, 1)
    ring(3, 2, 1)
    mids[1, 0] = near(1, 0)
    keep(0, 1)
    keep(1, 1)
    keep(1, 0)
    ring(2, 3, 0)
    ring(3, 3, 0)
    lows[0] = low_x(0, lows[0])
    ring(2, 3, 1)
    relay(0, 0, fars[0, 0], mids[0, 0])
    relay(0, 1, fars[0, 1], mids[0, 1])
    ring(3, 3, 1)
    lows[1] = low_x(1, lows[1])
    ring_end(2)
    lows[2] = low_part(2)
    relay(1, 0, fars[1, 0], mids[1, 0])
    relay(1, 1, fars[1, 1], mids[1, 1])
    fars[2, 1] = far(2, 1)
    fars[2, 0] = far(2, 0)
    mids[2, 1] = near(2, 1)
    ring_end(3)
    lows[3] = low_part(3)
    mids[2, 0] = near(2, 0)
    fars[3, 1] = far(3, 1)
    fars[3, 0] = far(3, 0)
    mids[3, 1] = near(3, 1)
    mids[3, 0] = near(3, 0)
    keep(2, 1)
    keep(2, 0)
    keep(3, 0)
    lows[0] = low_y(0, lows[0])
    keep(3, 1)
    lows[2] = low_x(2, lows[2])
    lows[1] = low_y(1, lows[1])
    relay(2, 0, fars[2, 0], mids[2, 0])
    relay(2, 1, fars[2, 1], mids[2, 1])
    lows[3] = low_x(3, lows[3])
    low_z(0, lows[0])
    arrived(b_c, bx)
    ends[0, 1] = collect(0, 1, mids[0, 1])
    relay(3, 1, fars[3, 1], mids[3, 1])
    relay(3, 0, fars[3, 0], mids[3, 0])
    ends[0, 0] = collect(0, 0, mids[0, 0])
    low_z(1, lows[1])
    ends[1, 0] = collect(1, 0, mids[1, 0])
    ends[1, 1] = collect(1, 1, mids[1, 1])
    lows[2] = low_y(2, lows[2])
    lows[3] = low_y(3, lows[3])
    finish(0, 1, ends[0, 1])
    finish(0, 0, ends[0, 0])
    finish(1, 1, ends[1, 1])
    finish(1, 0, ends[1, 0])
    low_z(2, lows[2])
    ends[2, 1] = collect(2, 1, mids[2, 1])
    ends[2, 0] = collect(2, 0, mids[2, 0])
    low_z(3, lows[3])
    ends[3, 1] = collect(3, 1, mids[3, 1])
    ends[3, 0] = collect(3, 0, mids[3, 0])
    finish(2, 1, ends[2, 1])
    finish(2, 0, ends[2, 0])
    finish(3, 1, ends[3, 1])
    finish(3, 0, ends[3, 0])
    for group in (START, UP, RING, SUMS):
        gone(group, wf)
    gone(LOWS, own_n)


def body(tokens, query_weight, down, up, request_combination, task_ids, coefficient):
    hbm = pl.BlockSpec(memory_space=pl.ANY)
    vmem = pl.BlockSpec(memory_space=pltpu.VMEM)
    n_sem = 79
    return pl.pallas_call(
        kernel,
        out_shape=jax.ShapeDtypeStruct((64, 2048), BF16),
        in_specs=[hbm, hbm, hbm, hbm, vmem, vmem, vmem],
        out_specs=vmem,
        scratch_shapes=[
            pltpu.VMEM((NS, 2, 16, RS, KC), BF16),
            pltpu.VMEM((1024, 2048), BF16),
            pltpu.VMEM((4, 8, 4096), BF16),
            pltpu.VMEM((2, 4, 4, 8, 1024), BF16),
            pltpu.VMEM((2, 4, 64, HALF), BF16),
            pltpu.VMEM((2, 4, 64, HALF), BF16),
            pltpu.VMEM((1024, 128), F32),
            pltpu.VMEM((1024, 128), F32),
            pltpu.VMEM((NS, 8, SR), F32),
            pltpu.VMEM((NS, 3, 8, SR), F32),
            pltpu.VMEM((NS, 3, 8, SR), F32),
            pltpu.VMEM((NS, 8, SR), F32),
            pltpu.VMEM((NS, 8, 8, SR), BF16),
            pltpu.VMEM((NS, 2, CR, HALF), BF16),
            pltpu.VMEM((NS, 2, 2, CR, QUART), BF16),
            pltpu.VMEM((NS, 2, 2, CR, HALF), BF16),
            pltpu.VMEM((NS, 2, 2, CR, HALF), BF16),
            pltpu.VMEM((NS, 2, CR, HALF), F32),
            pltpu.VMEM((NS, 2, 3, RS, HALF), BF16),
            pltpu.VMEM((NS, 2, 3, RS, HALF), BF16),
            pltpu.SemaphoreType.DMA((5,)),
            pltpu.SemaphoreType.DMA((n_sem,)),
            pltpu.SemaphoreType.DMA((NS + 5,)),
        ],
        compiler_params=pltpu.CompilerParams(
            collective_id=0, has_side_effects=True, vmem_limit_bytes=67043328
        ),
    )(
        tokens.reshape(2, 2, NS, RS, KC),
        query_weight,
        down.reshape(8, 8, 16384),
        up.reshape(64, 16384),
        request_combination.reshape(1, 2048),
        task_ids.T,
        coefficient.T,
    )


def solution(mesh):
    placed = (
        P("tensor", "adapter"),
        P("adapter", "tensor"),
        P("adapter", None, None),
        P("adapter", None, None),
        P(),
        P(),
        P(),
    )
    return jax.shard_map(
        body, mesh=mesh, in_specs=placed, out_specs=P("adapter", "tensor"), check_vma=False
    )
```

```python
import math

import jax
import jax.numpy as jnp
from jax import lax
from jax.experimental import pallas as pl
from jax.experimental.pallas import tpu as pltpu
from jax.sharding import PartitionSpec as P

NS = 2
RS = 64 // NS
SR = 16 * RS
CR = 4 * RS
NR = 8 * RS
PB = 64 // RS
KC = 512
HALF = 1024
QUART = 512
TILE = 256
F32 = jnp.float32
BF16 = jnp.bfloat16


def kernel(
    tok_hbm, w_hbm, a_hbm, b_hbm, rows_ref, ids_ref, coef_ref,
    out_ref,
    tok, wf, a1, a2, bx, by,
    own_n, low_n, lt, lx, ly, low_own, low_all,
    s2, r2, s1, r1, acc, t1, q1,
    send_sem, recv_sem, local_sem,
):
    a_idx = lax.axis_index("adapter")
    z = lax.axis_index("tensor")
    x = a_idx // 8
    y = (a_idx // 2) % 4
    c = a_idx % 2
    other = 1 - c

    def dev(xx, yy, cc, zz):
        return {"adapter": (xx * 4 + yy) * 2 + cc, "tensor": zz}

    def x_peer(k):
        return dev((x + k) % 4, y, c, z)

    def y_peer(k):
        return dev(x, (y + k) % 4, c, z)

    def z_peer(k):
        return dev(x, y, c, (z + k) % 8)

    partner = dev(x, y, other, z)
    task = z % 4
    counter = [0, 0]
    sent = [0] * 5
    START, UP, RING, SUMS, LOWS = range(5)

    def arrival():
        counter[0] += 1
        return counter[0] - 1

    def go(src, dst, device, mark, group):
        pltpu.make_async_remote_copy(
            src, dst, send_sem.at[group], recv_sem.at[mark],
            device_id=device, device_id_type=pl.DeviceIdType.MESH,
        ).start()
        sent[group] += math.prod(src.shape) * src.dtype.itemsize

    def arrived(mark, ref):
        pltpu.make_async_remote_copy(
            ref, ref, send_sem.at[0], recv_sem.at[mark],
            device_id=partner, device_id_type=pl.DeviceIdType.MESH,
        ).wait_recv()

    def gone(group, ref):
        row = math.prod(ref.shape[1:]) * ref.dtype.itemsize
        part = ref.at[pl.ds(0, sent[group] // row)]
        pltpu.make_async_remote_copy(
            part, part, send_sem.at[group], recv_sem.at[0],
            device_id=partner, device_id_type=pl.DeviceIdType.MESH,
        ).wait_send()

    def local(src, dst):
        i = counter[1]
        counter[1] += 1
        copy = pltpu.make_async_copy(src, dst, local_sem.at[i])
        copy.start()
        return copy

    my_cols = pl.ds(pl.multiple_of(c * KC, KC), KC)
    tok_local = [
        local(tok_hbm.at[:, c, s], tok.at[s, c, pl.ds(2 * z, 2)]) for s in range(NS)
    ]
    a_wide = lambda xx: pl.ds(pl.multiple_of(xx * 4096, 4096), 4096)
    a_narrow = lambda yy: pl.ds(pl.multiple_of(yy * 1024, 1024), 1024)
    a_local = local(a_hbm.at[task, :, a_wide(x)], a1.at[x])
    b_cols = [pl.ds(pl.multiple_of(z * 2048 + h * HALF, HALF), HALF) for h in range(2)]
    b_local = [
        local(b_hbm.at[:, b_cols[0]], bx.at[c, x]),
        local(b_hbm.at[:, b_cols[1]], by.at[c, y]),
    ]
    w_local = local(w_hbm, wf.at[my_cols, :])

    barrier = pltpu.get_barrier_semaphore()
    peers = [partner]
    peers += [x_peer(k) for k in range(1, 4)] + [y_peer(k) for k in range(1, 4)]
    peers += [z_peer(k) for k in range(1, 8)]
    for peer in peers:
        pl.semaphore_signal(barrier, inc=1, device_id=peer, device_id_type=pl.DeviceIdType.MESH)

    pl.semaphore_wait(barrier, len(peers))

    tok_pre = [arrival() for _ in range(NS)]

    def exchange(s):
        go(tok_hbm.at[:, other, s], tok.at[s, c, pl.ds(2 * z, 2)], partner, tok_pre[s], START)

    a_x, w_pre, a_y, a_c, b_x, b_y, b_c = [arrival() for _ in range(7)]

    moving = {}

    def ring(s, k, u):
        half = c if u == 0 else other
        if k > 0:
            arrived(moving.pop((s, k - 1, u)), tok.at[s, 0, pl.ds(0, 4)])
        moving[s, k, u] = mark = arrival()
        if k < 3 or u == 0:
            src = tok.at[s, half, pl.ds(2 * ((z - k + 8) % 8), 2)]
            go(src, src, z_peer(1), mark, RING)
        if k < 3 or u == 1:
            src = tok.at[s, half, pl.ds(2 * ((z + k) % 8), 2)]
            go(src, src, z_peer(7), mark, RING)

    def ring_end(s):
        for u in range(2):
            arrived(moving.pop((s, 3, u)), tok.at[s, 0, pl.ds(0, 2)])

    near_block = [(z + 7 + j) % 8 for j in range(4)]

    def wide(halves):
        return jnp.concatenate(halves, axis=1)

    def low_part(s):
        af = a2[...].reshape(512, 1024)
        for v in range(NR // 128):
            blocks = near_block[PB * v:PB * (v + 1)]
            rhs = wide([
                jnp.concatenate(
                    [tok[s, kc, pl.ds(2 * b, 2)].reshape(2 * RS, KC) for b in blocks], axis=0
                )
                for kc in range(2)
            ])
            part = lax.dot_general(
                af, rhs, (((1,), (1,)), ((), ())), preferred_element_type=F32
            )
            total = jnp.zeros((16, 128), F32)
            for g in range(32):
                o = ((g % 4) * 4 + (g // 4) % 4) * 2 + g // 16
                total += jnp.where(near_owner[s][v] == o, part[16 * g:16 * (g + 1)], 0.0)
            lt[s, :, 128 * v:128 * (v + 1)] = total
        mark = arrival()
        for k in range(1, 4):
            go(lt.at[s], lx.at[s, k - 1], x_peer(k), mark, LOWS)
        return mark

    def low_x(s, mark):
        arrived(mark, lx.at[s])
        low_own[s] = (lt[s] + lx[s, 0]) + (lx[s, 1] + lx[s, 2])
        mark = arrival()
        for k in range(1, 4):
            go(low_own.at[s], ly.at[s, k - 1], y_peer(k), mark, LOWS)
        return mark

    def low_y(s, mark):
        arrived(mark, ly.at[s])
        total = (low_own[s] + ly[s, 0]) + (ly[s, 1] + ly[s, 2])
        low_all[s, z] = (total * weight[s]).astype(BF16)
        mark = arrival()
        for k in (4, 3, 5, 2, 6, 1, 7):
            go(low_all.at[s, z], low_all.at[s, z], z_peer(k), mark, LOWS)
        return mark

    def low_z(s, mark):
        arrived(mark, low_all.at[s, pl.ds(0, 7)])
        group = lax.broadcasted_iota(jnp.int32, (16, 128), 1) // (2 * RS)
        for m in range(8 // PB):
            parts = []
            for t in range(4):
                piece = jnp.zeros((16, 128), F32)
                for bl in range(PB):
                    b = PB * m + bl
                    zz, j = [
                        (v % 8, b - v + 1) for v in range(b - 2, b + 2) if v % 4 == t
                    ][0]
                    lanes = slice(128 * (j // PB), 128 * (j // PB) + 128)
                    moved = pltpu.roll(
                        low_all[s, zz, :, lanes].astype(F32), (2 * RS * (bl - j % PB)) % 128, 1
                    )
                    piece = jnp.where(group == bl, moved, piece)
                parts.append(piece)
            at = s * SR + 128 * m
            low_n[at:at + 128, :] = jnp.transpose(jnp.concatenate(parts + parts, axis=0))

    place = (x, y)
    ring_peer = (x_peer, y_peer)

    def cut(n):
        return slice(n * TILE, (n + 1) * TILE)

    lo, hi = pl.ds(0, QUART), pl.ds(QUART, QUART)

    def dots(s, h, q, first, count, emit):
        if h == 0:
            lhs = wide([tok[s, kc, pl.ds(4 * q, 4)].reshape(CR, KC) for kc in range(2)])
        else:
            lhs = wide([
                jnp.concatenate([tok[s, kc, 4 * j + q] for j in range(4)], axis=0)
                for kc in range(2)
            ])
        for n in range(first, first + count):
            cols = slice(h * HALF + n * TILE, h * HALF + (n + 1) * TILE)
            emit(n, jnp.dot(lhs, wf[:, cols], preferred_element_type=F32))

    def far(s, h):
        def put(n, v):
            s2[s, h, :, cut(n)] = v.astype(BF16)
        dots(s, h, (place[h] + 2) % 4, 0, 4, put)
        mark = arrival()
        go(s2.at[s, h, :, lo], r2.at[s, h, 0], ring_peer[h](1), mark, SUMS)
        go(s2.at[s, h, :, hi], r2.at[s, h, 1], ring_peer[h](3), mark, SUMS)
        return mark

    def near(s, h):
        def put_r(n, v):
            s1[s, h, 0, :, cut(n)] = v.astype(BF16)
        def put_l(n, v):
            s1[s, h, 1, :, cut(n)] = v.astype(BF16)
        mark = arrival()
        dots(s, h, (place[h] + 1) % 4, 2, 2, put_r)
        go(s1.at[s, h, 0, :, hi], r1.at[s, h, 0, :, hi], ring_peer[h](1), mark, SUMS)
        dots(s, h, (place[h] + 3) % 4, 0, 2, put_l)
        go(s1.at[s, h, 1, :, lo], r1.at[s, h, 1, :, lo], ring_peer[h](3), mark, SUMS)
        return mark

    def keep(s, h):
        def put(n, v):
            acc[s, h, :, cut(n)] = v
        dots(s, h, place[h], 0, 4, put)

    def relay(s, h, ready, mark):
        arrived(ready, r2.at[s, h])
        def add_r(n, v):
            s1[s, h, 0, :, cut(n)] = (v + r2[s, h, 0, :, cut(n)].astype(F32)).astype(BF16)
        def add_l(n, v):
            s1[s, h, 1, :, cut(n)] = (v + r2[s, h, 1, :, cut(n - 2)].astype(F32)).astype(BF16)
        dots(s, h, (place[h] + 1) % 4, 0, 2, add_r)
        go(s1.at[s, h, 0, :, lo], r1.at[s, h, 0, :, lo], ring_peer[h](1), mark, SUMS)
        dots(s, h, (place[h] + 3) % 4, 2, 2, add_l)
        go(s1.at[s, h, 1, :, hi], r1.at[s, h, 1, :, hi], ring_peer[h](3), mark, SUMS)

    lane = lax.broadcasted_iota(jnp.int32, (CR, 128), 1)

    def masked(s, h):
        if h == 0:
            at = pl.ds(pl.multiple_of(s * SR + x * CR, CR), CR)
            ow, lw = own_n[at, :], low_n[at, :]
        else:
            ats = [pl.ds(pl.multiple_of(s * SR + (4 * j + y) * RS, RS), RS) for j in range(4)]
            ow = jnp.concatenate([own_n[at, :] for at in ats], axis=0)
            lw = jnp.concatenate([low_n[at, :] for at in ats], axis=0)
        pieces = []
        for cc in range(2):
            for m in range(2):
                if h == 0:
                    o0, step = ((2 * m) * 4 + y) * 2 + cc, 8
                else:
                    o0, step = (x * 4 + 2 * m) * 2 + cc, 2
                want = jnp.where(lane < 64, o0, o0 + step).astype(F32)
                pieces.append(jnp.where(ow == want, lw, 0.0).astype(BF16))
        return jnp.concatenate(pieces, axis=1)

    place2 = (y, x)
    peer2 = (y_peer, x_peer)

    def block(h, q):
        return pl.ds(pl.multiple_of(q * RS, RS), RS)

    def collect(s, h, mark):
        arrived(mark, r1.at[s, h])
        lhs = masked(s, h)
        up = (bx, by)[h]
        for n in range(4):
            delta = jnp.dot(
                lhs, up[:, :, :, cut(n)].reshape(512, TILE), preferred_element_type=F32
            )
            acc[s, h, :, cut(n)] = (acc[s, h, :, cut(n)] + delta) + (
                r1[s, h, 0, :, cut(n)].astype(F32) + r1[s, h, 1, :, cut(n)].astype(F32)
            )
        mark = arrival()
        for k in (2, 1, 3):
            t1[s, h, k - 1] = acc[s, h, block(h, (place2[h] + k) % 4), :].astype(BF16)
            go(t1.at[s, h, k - 1], q1.at[s, h, k - 1], peer2[h](k), mark, SUMS)
        return mark

    def finish(s, h, mark):
        arrived(mark, q1.at[s, h])
        out_ref[s * RS:(s + 1) * RS, h * HALF:(h + 1) * HALF] = (
            (acc[s, h, block(h, place2[h]), :] + q1[s, h, 0].astype(F32))
            + (q1[s, h, 1].astype(F32) + q1[s, h, 2].astype(F32))
        ).astype(BF16)

    lows, fars, mids, ends = {}, {}, {}, {}
    for cp in tok_local:
        cp.wait()
    ring(0, 0, 0)
    for s in range(NS):
        exchange(s)
    for k in range(1, 4):
        go(a_hbm.at[task, :, a_wide((x + k) % 4)], a1.at[x], x_peer(k), a_x, START)
    go(w_hbm, wf.at[my_cols, :], partner, w_pre, START)
    lane8 = lax.broadcasted_iota(jnp.int32, (8, 128), 1)

    def numbers(s, ds):
        piece = jnp.zeros((8, 128), jnp.int32)
        for j, d in enumerate(ds):
            raw = rows_ref[:, pl.ds(pl.multiple_of(128 * d, 128), 128)]
            raw = jnp.broadcast_to(raw, (8, 128))
            shift = (RS * j - RS * s + 256 - 64 * c) % 128
            piece = jnp.where(lane8 // RS == j, pltpu.roll(raw, shift, 1), piece)
        return piece[0:1]

    combo = lax.broadcasted_iota(jnp.int32, (4, 512), 1)
    hit = (ids_ref[...] - (combo // 16) * 4) == task
    table = 0.25 * jnp.sum(jnp.where(hit, coef_ref[...], 0).astype(F32), axis=0, keepdims=True)
    column = jnp.concatenate(
        [
            jnp.transpose(jnp.broadcast_to(table[:, 128 * k:128 * (k + 1)], (128, 128)))
            for k in range(4)
        ],
        axis=0,
    )
    number = lax.broadcasted_iota(jnp.int32, (512, 128), 0)
    per = 128 // RS
    near_d = [2 * b + jj for b in near_block for jj in range(2)]
    near_rows = [
        [numbers(s, near_d[per * v:per * (v + 1)]) for v in range(NR // 128)] for s in range(NS)
    ]
    near_owner = [[rows // 16 for rows in stage] for stage in near_rows]
    weight = [
        jnp.concatenate(
            [
                jnp.sum(jnp.where(number == rows, column, 0.0), axis=0, keepdims=True)
                for rows in stage
            ],
            axis=1,
        )
        for stage in near_rows
    ]
    arrived(tok_pre[0], tok.at[0, 0, pl.ds(0, 2)])
    ring(0, 0, 1)
    for s in range(NS):
        for m in range(SR // 128):
            owner = numbers(s, range(per * m, per * (m + 1))) // 16
            tile = jnp.broadcast_to(owner.astype(F32), (128, 128))
            at = s * SR + 128 * m
            own_n[at:at + 128, :] = jnp.transpose(tile)
    ring(0, 1, 0)
    ring(0, 1, 1)
    ring(0, 2, 0)
    ring(1, 0, 0)
    a_local.wait()
    arrived(a_x, a1.at[pl.ds(0, 3)])
    a_own = local(a1.at[:, :, a_narrow(y)], a2.at[c, y])
    for k in range(1, 4):
        go(a1.at[:, :, a_narrow((y + k) % 4)], a2.at[c, y], y_peer(k), a_y, START)
    for k in range(1, 4):
        go(b_hbm.at[:, b_cols[0]], bx.at[c, x], x_peer(k), b_x, UP)
        go(b_hbm.at[:, b_cols[1]], by.at[c, y], y_peer(k), b_y, UP)
    ring(0, 2, 1)
    arrived(tok_pre[1], tok.at[1, 0, pl.ds(0, 2)])
    ring(1, 0, 1)
    ring(0, 3, 0)
    ring(1, 1, 0)
    ring(0, 3, 1)
    ring(1, 1, 1)
    a_own.wait()
    arrived(a_y, a2.at[0, pl.ds(0, 3)])
    go(a2.at[c], a2.at[c], partner, a_c, START)
    ring(1, 2, 0)
    w_local.wait()
    arrived(w_pre, wf.at[pl.ds(0, KC)])
    ring_end(0)
    fars[0, 0] = far(0, 0)
    fars[0, 1] = far(0, 1)
    mids[0, 0] = near(0, 0)
    mids[0, 1] = near(0, 1)
    keep(0, 1)
    keep(0, 0)
    arrived(a_c, a2.at[0])
    lows[0] = low_part(0)
    ring(1, 2, 1)
    lows[1] = low_part(1)
    ring(1, 3, 0)
    for cp in b_local:
        cp.wait()
    arrived(b_x, bx.at[0, pl.ds(0, 3)])
    arrived(b_y, by.at[0, pl.ds(0, 3)])
    for ref in (bx, by):
        go(ref.at[c], ref.at[c], partner, b_c, UP)
    relay(0, 0, fars[0, 0], mids[0, 0])
    ring(1, 3, 1)
    relay(0, 1, fars[0, 1], mids[0, 1])
    ring_end(1)
    fars[1, 1] = far(1, 1)
    fars[1, 0] = far(1, 0)
    lows[0] = low_x(0, lows[0])
    mids[1, 1] = near(1, 1)
    lows[1] = low_x(1, lows[1])
    mids[1, 0] = near(1, 0)
    keep(1, 0)
    keep(1, 1)
    relay(1, 1, fars[1, 1], mids[1, 1])
    relay(1, 0, fars[1, 0], mids[1, 0])
    lows[0] = low_y(0, lows[0])
    lows[1] = low_y(1, lows[1])
    low_z(0, lows[0])
    arrived(b_c, bx)
    ends[0, 0] = collect(0, 0, mids[0, 0])
    ends[0, 1] = collect(0, 1, mids[0, 1])
    low_z(1, lows[1])
    ends[1, 1] = collect(1, 1, mids[1, 1])
    ends[1, 0] = collect(1, 0, mids[1, 0])
    finish(0, 0, ends[0, 0])
    finish(0, 1, ends[0, 1])
    finish(1, 1, ends[1, 1])
    finish(1, 0, ends[1, 0])
    for group in (START, UP, RING, SUMS):
        gone(group, wf)
    gone(LOWS, own_n)


def body(tokens, query_weight, down, up, request_combination, task_ids, coefficient):
    hbm = pl.BlockSpec(memory_space=pl.ANY)
    vmem = pl.BlockSpec(memory_space=pltpu.VMEM)
    n_sem = 43
    return pl.pallas_call(
        kernel,
        out_shape=jax.ShapeDtypeStruct((64, 2048), BF16),
        in_specs=[hbm, hbm, hbm, hbm, vmem, vmem, vmem],
        out_specs=vmem,
        scratch_shapes=[
            pltpu.VMEM((NS, 2, 16, RS, KC), BF16),
            pltpu.VMEM((1024, 2048), BF16),
            pltpu.VMEM((4, 16, 4096), BF16),
            pltpu.VMEM((2, 4, 4, 16, 1024), BF16),
            pltpu.VMEM((2, 4, 64, HALF), BF16),
            pltpu.VMEM((2, 4, 64, HALF), BF16),
            pltpu.VMEM((1024, 128), F32),
            pltpu.VMEM((1024, 128), F32),
            pltpu.VMEM((NS, 16, NR), F32),
            pltpu.VMEM((NS, 3, 16, NR), F32),
            pltpu.VMEM((NS, 3, 16, NR), F32),
            pltpu.VMEM((NS, 16, NR), F32),
            pltpu.VMEM((NS, 8, 16, NR), BF16),
            pltpu.VMEM((NS, 2, CR, HALF), BF16),
            pltpu.VMEM((NS, 2, 2, CR, QUART), BF16),
            pltpu.VMEM((NS, 2, 2, CR, HALF), BF16),
            pltpu.VMEM((NS, 2, 2, CR, HALF), BF16),
            pltpu.VMEM((NS, 2, CR, HALF), F32),
            pltpu.VMEM((NS, 2, 3, RS, HALF), BF16),
            pltpu.VMEM((NS, 2, 3, RS, HALF), BF16),
            pltpu.SemaphoreType.DMA((5,)),
            pltpu.SemaphoreType.DMA((n_sem,)),
            pltpu.SemaphoreType.DMA((NS + 5,)),
        ],
        compiler_params=pltpu.CompilerParams(
            collective_id=0, has_side_effects=True, vmem_limit_bytes=67043328
        ),
    )(
        tokens.reshape(2, 2, NS, RS, KC),
        query_weight,
        down,
        up.reshape(64, 16384),
        request_combination.reshape(1, 2048),
        task_ids.T,
        coefficient.T,
    )


def solution(mesh):
    placed = (
        P("tensor", "adapter"),
        P("adapter", "tensor"),
        P("adapter", None, None),
        P("adapter", None, None),
        P(),
        P(),
        P(),
    )
    return jax.shard_map(
        body, mesh=mesh, in_specs=placed, out_specs=P("adapter", "tensor"), check_vma=False
    )
```

```python
import math

import jax
import jax.numpy as jnp
from jax import lax
from jax.experimental import pallas as pl
from jax.experimental.pallas import tpu as pltpu
from jax.sharding import PartitionSpec as P

NS = 2
RS = 64 // NS
SR = 16 * RS
CR = 4 * RS
NR = 8 * RS
PB = 64 // RS
KC = 512
HALF = 1024
QUART = 512
TILE = 256
F32 = jnp.float32
BF16 = jnp.bfloat16


def kernel(
    tok_hbm, w_hbm, a_hbm, b_hbm, rows_ref, ids_ref, coef_ref,
    out_ref,
    tok, wf, a1, a2, bx, by,
    own_n, low_n, lt, lx, ly, low_own, low_all,
    s2, r2, s1, r1, acc, t1, q1,
    send_sem, recv_sem, local_sem,
):
    a_idx = lax.axis_index("adapter")
    z = lax.axis_index("tensor")
    x = a_idx // 8
    y = (a_idx // 2) % 4
    c = a_idx % 2
    other = 1 - c

    def dev(xx, yy, cc, zz):
        return {"adapter": (xx * 4 + yy) * 2 + cc, "tensor": zz}

    def x_peer(k):
        return dev((x + k) % 4, y, c, z)

    def y_peer(k):
        return dev(x, (y + k) % 4, c, z)

    def z_peer(k):
        return dev(x, y, c, (z + k) % 8)

    partner = dev(x, y, other, z)
    task = z % 4
    counter = [0, 0]
    sent = [0] * 5
    START, UP, RING, SUMS, LOWS = range(5)

    def arrival():
        counter[0] += 1
        return counter[0] - 1

    def go(src, dst, device, mark, group):
        pltpu.make_async_remote_copy(
            src, dst, send_sem.at[group], recv_sem.at[mark],
            device_id=device, device_id_type=pl.DeviceIdType.MESH,
        ).start()
        sent[group] += math.prod(src.shape) * src.dtype.itemsize

    def arrived(mark, ref):
        pltpu.make_async_remote_copy(
            ref, ref, send_sem.at[0], recv_sem.at[mark],
            device_id=partner, device_id_type=pl.DeviceIdType.MESH,
        ).wait_recv()

    def gone(group, ref):
        row = math.prod(ref.shape[1:]) * ref.dtype.itemsize
        part = ref.at[pl.ds(0, sent[group] // row)]
        pltpu.make_async_remote_copy(
            part, part, send_sem.at[group], recv_sem.at[0],
            device_id=partner, device_id_type=pl.DeviceIdType.MESH,
        ).wait_send()

    def local(src, dst):
        i = counter[1]
        counter[1] += 1
        copy = pltpu.make_async_copy(src, dst, local_sem.at[i])
        copy.start()
        return copy

    my_cols = pl.ds(pl.multiple_of(c * KC, KC), KC)
    tok_local = [
        local(tok_hbm.at[:, c, s], tok.at[s, c, pl.ds(2 * z, 2)]) for s in range(NS)
    ]
    a_wide = lambda xx: pl.ds(pl.multiple_of(xx * 4096, 4096), 4096)
    a_narrow = lambda yy: pl.ds(pl.multiple_of(yy * 1024, 1024), 1024)
    a_local = local(a_hbm.at[task, :, a_wide(x)], a1.at[x])
    b_cols = [pl.ds(pl.multiple_of(z * 2048 + h * HALF, HALF), HALF) for h in range(2)]
    b_local = [
        local(b_hbm.at[:, b_cols[0]], bx.at[c, x]),
        local(b_hbm.at[:, b_cols[1]], by.at[c, y]),
    ]
    w_local = local(w_hbm, wf.at[my_cols, :])

    barrier = pltpu.get_barrier_semaphore()
    peers = [partner]
    peers += [x_peer(k) for k in range(1, 4)] + [y_peer(k) for k in range(1, 4)]
    peers += [z_peer(k) for k in range(1, 8)]
    for peer in peers:
        pl.semaphore_signal(barrier, inc=1, device_id=peer, device_id_type=pl.DeviceIdType.MESH)

    pl.semaphore_wait(barrier, len(peers))

    tok_pre = [arrival() for _ in range(NS)]

    def exchange(s):
        go(tok_hbm.at[:, other, s], tok.at[s, c, pl.ds(2 * z, 2)], partner, tok_pre[s], START)

    a_x, w_pre, a_y, a_c, b_x, b_y, b_c = [arrival() for _ in range(7)]

    moving = {}

    def ring(s, k, u):
        half = c if u == 0 else other
        if k > 0:
            arrived(moving.pop((s, k - 1, u)), tok.at[s, 0, pl.ds(0, 4)])
        moving[s, k, u] = mark = arrival()
        if k < 3 or u == 0:
            src = tok.at[s, half, pl.ds(2 * ((z - k + 8) % 8), 2)]
            go(src, src, z_peer(1), mark, RING)
        if k < 3 or u == 1:
            src = tok.at[s, half, pl.ds(2 * ((z + k) % 8), 2)]
            go(src, src, z_peer(7), mark, RING)

    def ring_end(s):
        for u in range(2):
            arrived(moving.pop((s, 3, u)), tok.at[s, 0, pl.ds(0, 2)])

    near_block = [(z + 7 + j) % 8 for j in range(4)]

    def wide(halves):
        return jnp.concatenate(halves, axis=1)

    def low_part(s):
        af = a2[...].reshape(512, 1024)
        for v in range(NR // 128):
            blocks = near_block[PB * v:PB * (v + 1)]
            rhs = wide([
                jnp.concatenate(
                    [tok[s, kc, pl.ds(2 * b, 2)].reshape(2 * RS, KC) for b in blocks], axis=0
                )
                for kc in range(2)
            ])
            part = lax.dot_general(
                af, rhs, (((1,), (1,)), ((), ())), preferred_element_type=F32
            )
            total = jnp.zeros((16, 128), F32)
            for g in range(32):
                o = ((g % 4) * 4 + (g // 4) % 4) * 2 + g // 16
                total += jnp.where(near_owner[s][v] == o, part[16 * g:16 * (g + 1)], 0.0)
            lt[s, :, 128 * v:128 * (v + 1)] = total
        mark = arrival()
        for k in range(1, 4):
            go(lt.at[s], lx.at[s, k - 1], x_peer(k), mark, LOWS)
        return mark

    def low_x(s, mark):
        arrived(mark, lx.at[s])
        low_own[s] = (lt[s] + lx[s, 0]) + (lx[s, 1] + lx[s, 2])
        mark = arrival()
        for k in range(1, 4):
            go(low_own.at[s], ly.at[s, k - 1], y_peer(k), mark, LOWS)
        return mark

    def low_y(s, mark):
        arrived(mark, ly.at[s])
        total = (low_own[s] + ly[s, 0]) + (ly[s, 1] + ly[s, 2])
        low_all[s, z] = (total * weight[s]).astype(BF16)
        mark = arrival()
        for k in (4, 3, 5, 2, 6, 1, 7):
            go(low_all.at[s, z], low_all.at[s, z], z_peer(k), mark, LOWS)
        return mark

    def low_z(s, mark):
        arrived(mark, low_all.at[s, pl.ds(0, 7)])
        group = lax.broadcasted_iota(jnp.int32, (16, 128), 1) // (2 * RS)
        for m in range(8 // PB):
            parts = []
            for t in range(4):
                piece = jnp.zeros((16, 128), F32)
                for bl in range(PB):
                    b = PB * m + bl
                    zz, j = [
                        (v % 8, b - v + 1) for v in range(b - 2, b + 2) if v % 4 == t
                    ][0]
                    lanes = slice(128 * (j // PB), 128 * (j // PB) + 128)
                    moved = pltpu.roll(
                        low_all[s, zz, :, lanes].astype(F32), (2 * RS * (bl - j % PB)) % 128, 1
                    )
                    piece = jnp.where(group == bl, moved, piece)
                parts.append(piece)
            at = s * SR + 128 * m
            low_n[at:at + 128, :] = jnp.transpose(jnp.concatenate(parts + parts, axis=0))

    place = (x, y)
    ring_peer = (x_peer, y_peer)

    def cut(n):
        return slice(n * TILE, (n + 1) * TILE)

    lo, hi = pl.ds(0, QUART), pl.ds(QUART, QUART)

    def dots(s, h, q, first, count, emit):
        if h == 0:
            lhs = wide([tok[s, kc, pl.ds(4 * q, 4)].reshape(CR, KC) for kc in range(2)])
        else:
            lhs = wide([
                jnp.concatenate([tok[s, kc, 4 * j + q] for j in range(4)], axis=0)
                for kc in range(2)
            ])
        for n in range(first, first + count):
            cols = slice(h * HALF + n * TILE, h * HALF + (n + 1) * TILE)
            emit(n, jnp.dot(lhs, wf[:, cols], preferred_element_type=F32))

    def far(s, h):
        def put(n, v):
            s2[s, h, :, cut(n)] = v.astype(BF16)
        dots(s, h, (place[h] + 2) % 4, 0, 4, put)
        mark = arrival()
        go(s2.at[s, h, :, lo], r2.at[s, h, 0], ring_peer[h](1), mark, SUMS)
        go(s2.at[s, h, :, hi], r2.at[s, h, 1], ring_peer[h](3), mark, SUMS)
        return mark

    def near(s, h):
        def put_r(n, v):
            s1[s, h, 0, :, cut(n)] = v.astype(BF16)
        def put_l(n, v):
            s1[s, h, 1, :, cut(n)] = v.astype(BF16)
        mark = arrival()
        dots(s, h, (place[h] + 1) % 4, 2, 2, put_r)
        go(s1.at[s, h, 0, :, hi], r1.at[s, h, 0, :, hi], ring_peer[h](1), mark, SUMS)
        dots(s, h, (place[h] + 3) % 4, 0, 2, put_l)
        go(s1.at[s, h, 1, :, lo], r1.at[s, h, 1, :, lo], ring_peer[h](3), mark, SUMS)
        return mark

    def keep(s, h):
        def put(n, v):
            acc[s, h, :, cut(n)] = v
        dots(s, h, place[h], 0, 4, put)

    def relay(s, h, ready, mark):
        arrived(ready, r2.at[s, h])
        def add_r(n, v):
            s1[s, h, 0, :, cut(n)] = (v + r2[s, h, 0, :, cut(n)].astype(F32)).astype(BF16)
        def add_l(n, v):
            s1[s, h, 1, :, cut(n)] = (v + r2[s, h, 1, :, cut(n - 2)].astype(F32)).astype(BF16)
        dots(s, h, (place[h] + 1) % 4, 0, 2, add_r)
        go(s1.at[s, h, 0, :, lo], r1.at[s, h, 0, :, lo], ring_peer[h](1), mark, SUMS)
        dots(s, h, (place[h] + 3) % 4, 2, 2, add_l)
        go(s1.at[s, h, 1, :, hi], r1.at[s, h, 1, :, hi], ring_peer[h](3), mark, SUMS)

    lane = lax.broadcasted_iota(jnp.int32, (CR, 128), 1)

    def masked(s, h):
        if h == 0:
            at = pl.ds(pl.multiple_of(s * SR + x * CR, CR), CR)
            ow, lw = own_n[at, :], low_n[at, :]
        else:
            ats = [pl.ds(pl.multiple_of(s * SR + (4 * j + y) * RS, RS), RS) for j in range(4)]
            ow = jnp.concatenate([own_n[at, :] for at in ats], axis=0)
            lw = jnp.concatenate([low_n[at, :] for at in ats], axis=0)
        pieces = []
        for cc in range(2):
            for m in range(2):
                if h == 0:
                    o0, step = ((2 * m) * 4 + y) * 2 + cc, 8
                else:
                    o0, step = (x * 4 + 2 * m) * 2 + cc, 2
                want = jnp.where(lane < 64, o0, o0 + step).astype(F32)
                pieces.append(jnp.where(ow == want, lw, 0.0).astype(BF16))
        return jnp.concatenate(pieces, axis=1)

    place2 = (y, x)
    peer2 = (y_peer, x_peer)

    def block(h, q):
        return pl.ds(pl.multiple_of(q * RS, RS), RS)

    def collect(s, h, mark):
        arrived(mark, r1.at[s, h])
        lhs = masked(s, h)
        up = (bx, by)[h]
        for n in range(4):
            delta = jnp.dot(
                lhs, up[:, :, :, cut(n)].reshape(512, TILE), preferred_element_type=F32
            )
            acc[s, h, :, cut(n)] = (acc[s, h, :, cut(n)] + delta) + (
                r1[s, h, 0, :, cut(n)].astype(F32) + r1[s, h, 1, :, cut(n)].astype(F32)
            )
        mark = arrival()
        for k in (2, 1, 3):
            t1[s, h, k - 1] = acc[s, h, block(h, (place2[h] + k) % 4), :].astype(BF16)
            go(t1.at[s, h, k - 1], q1.at[s, h, k - 1], peer2[h](k), mark, SUMS)
        return mark

    def finish(s, h, mark):
        arrived(mark, q1.at[s, h])
        out_ref[s * RS:(s + 1) * RS, h * HALF:(h + 1) * HALF] = (
            (acc[s, h, block(h, place2[h]), :] + q1[s, h, 0].astype(F32))
            + (q1[s, h, 1].astype(F32) + q1[s, h, 2].astype(F32))
        ).astype(BF16)

    lows, fars, mids, ends = {}, {}, {}, {}
    for cp in tok_local:
        cp.wait()
    ring(0, 0, 0)
    for s in range(NS):
        exchange(s)
    for k in range(1, 4):
        go(a_hbm.at[task, :, a_wide((x + k) % 4)], a1.at[x], x_peer(k), a_x, START)
    go(w_hbm, wf.at[my_cols, :], partner, w_pre, START)
    lane8 = lax.broadcasted_iota(jnp.int32, (8, 128), 1)

    def numbers(s, ds):
        piece = jnp.zeros((8, 128), jnp.int32)
        for j, d in enumerate(ds):
            raw = rows_ref[:, pl.ds(pl.multiple_of(128 * d, 128), 128)]
            raw = jnp.broadcast_to(raw, (8, 128))
            shift = (RS * j - RS * s + 256 - 64 * c) % 128
            piece = jnp.where(lane8 // RS == j, pltpu.roll(raw, shift, 1), piece)
        return piece[0:1]

    combo = lax.broadcasted_iota(jnp.int32, (4, 512), 1)
    hit = (ids_ref[...] - (combo // 16) * 4) == task
    table = 0.25 * jnp.sum(jnp.where(hit, coef_ref[...], 0).astype(F32), axis=0, keepdims=True)
    column = jnp.concatenate(
        [
            jnp.transpose(jnp.broadcast_to(table[:, 128 * k:128 * (k + 1)], (128, 128)))
            for k in range(4)
        ],
        axis=0,
    )
    number = lax.broadcasted_iota(jnp.int32, (512, 128), 0)
    per = 128 // RS
    near_d = [2 * b + jj for b in near_block for jj in range(2)]
    near_rows = [
        [numbers(s, near_d[per * v:per * (v + 1)]) for v in range(NR // 128)] for s in range(NS)
    ]
    near_owner = [[rows // 16 for rows in stage] for stage in near_rows]
    weight = [
        jnp.concatenate(
            [
                jnp.sum(jnp.where(number == rows, column, 0.0), axis=0, keepdims=True)
                for rows in stage
            ],
            axis=1,
        )
        for stage in near_rows
    ]
    arrived(tok_pre[0], tok.at[0, 0, pl.ds(0, 2)])
    ring(0, 0, 1)
    for s in range(NS):
        for m in range(SR // 128):
            owner = numbers(s, range(per * m, per * (m + 1))) // 16
            tile = jnp.broadcast_to(owner.astype(F32), (128, 128))
            at = s * SR + 128 * m
            own_n[at:at + 128, :] = jnp.transpose(tile)
    ring(0, 1, 0)
    ring(0, 1, 1)
    ring(0, 2, 0)
    ring(1, 0, 0)
    a_local.wait()
    arrived(a_x, a1.at[pl.ds(0, 3)])
    a_own = local(a1.at[:, :, a_narrow(y)], a2.at[c, y])
    for k in range(1, 4):
        go(a1.at[:, :, a_narrow((y + k) % 4)], a2.at[c, y], y_peer(k), a_y, START)
    for k in range(1, 4):
        go(b_hbm.at[:, b_cols[0]], bx.at[c, x], x_peer(k), b_x, UP)
        go(b_hbm.at[:, b_cols[1]], by.at[c, y], y_peer(k), b_y, UP)
    ring(0, 2, 1)
    arrived(tok_pre[1], tok.at[1, 0, pl.ds(0, 2)])
    ring(1, 0, 1)
    ring(0, 3, 0)
    ring(1, 1, 0)
    ring(0, 3, 1)
    ring(1, 1, 1)
    a_own.wait()
    arrived(a_y, a2.at[0, pl.ds(0, 3)])
    go(a2.at[c], a2.at[c], partner, a_c, START)
    ring(1, 2, 0)
    w_local.wait()
    arrived(w_pre, wf.at[pl.ds(0, KC)])
    ring_end(0)
    fars[0, 0] = far(0, 0)
    fars[0, 1] = far(0, 1)
    mids[0, 1] = near(0, 1)
    arrived(a_c, a2.at[0])
    lows[0] = low_part(0)
    mids[0, 0] = near(0, 0)
    keep(0, 0)
    keep(0, 1)
    ring(1, 2, 1)
    lows[1] = low_part(1)
    for cp in b_local:
        cp.wait()
    arrived(b_x, bx.at[0, pl.ds(0, 3)])
    arrived(b_y, by.at[0, pl.ds(0, 3)])
    for ref in (bx, by):
        go(ref.at[c], ref.at[c], partner, b_c, UP)
    ring(1, 3, 0)
    relay(0, 0, fars[0, 0], mids[0, 0])
    relay(0, 1, fars[0, 1], mids[0, 1])
    ring(1, 3, 1)
    lows[0] = low_x(0, lows[0])
    lows[1] = low_x(1, lows[1])
    ring_end(1)
    fars[1, 1] = far(1, 1)
    fars[1, 0] = far(1, 0)
    mids[1, 1] = near(1, 1)
    mids[1, 0] = near(1, 0)
    keep(1, 0)
    keep(1, 1)
    lows[0] = low_y(0, lows[0])
    lows[1] = low_y(1, lows[1])
    relay(1, 1, fars[1, 1], mids[1, 1])
    relay(1, 0, fars[1, 0], mids[1, 0])
    low_z(0, lows[0])
    arrived(b_c, bx)
    ends[0, 1] = collect(0, 1, mids[0, 1])
    ends[0, 0] = collect(0, 0, mids[0, 0])
    low_z(1, lows[1])
    ends[1, 1] = collect(1, 1, mids[1, 1])
    ends[1, 0] = collect(1, 0, mids[1, 0])
    finish(0, 1, ends[0, 1])
    finish(0, 0, ends[0, 0])
    finish(1, 1, ends[1, 1])
    finish(1, 0, ends[1, 0])
    for group in (START, UP, RING, SUMS):
        gone(group, wf)
    gone(LOWS, own_n)


def body(tokens, query_weight, down, up, request_combination, task_ids, coefficient):
    hbm = pl.BlockSpec(memory_space=pl.ANY)
    vmem = pl.BlockSpec(memory_space=pltpu.VMEM)
    n_sem = 43
    return pl.pallas_call(
        kernel,
        out_shape=jax.ShapeDtypeStruct((64, 2048), BF16),
        in_specs=[hbm, hbm, hbm, hbm, vmem, vmem, vmem],
        out_specs=vmem,
        scratch_shapes=[
            pltpu.VMEM((NS, 2, 16, RS, KC), BF16),
            pltpu.VMEM((1024, 2048), BF16),
            pltpu.VMEM((4, 16, 4096), BF16),
            pltpu.VMEM((2, 4, 4, 16, 1024), BF16),
            pltpu.VMEM((2, 4, 64, HALF), BF16),
            pltpu.VMEM((2, 4, 64, HALF), BF16),
            pltpu.VMEM((1024, 128), F32),
            pltpu.VMEM((1024, 128), F32),
            pltpu.VMEM((NS, 16, NR), F32),
            pltpu.VMEM((NS, 3, 16, NR), F32),
            pltpu.VMEM((NS, 3, 16, NR), F32),
            pltpu.VMEM((NS, 16, NR), F32),
            pltpu.VMEM((NS, 8, 16, NR), BF16),
            pltpu.VMEM((NS, 2, CR, HALF), BF16),
            pltpu.VMEM((NS, 2, 2, CR, QUART), BF16),
            pltpu.VMEM((NS, 2, 2, CR, HALF), BF16),
            pltpu.VMEM((NS, 2, 2, CR, HALF), BF16),
            pltpu.VMEM((NS, 2, CR, HALF), F32),
            pltpu.VMEM((NS, 2, 3, RS, HALF), BF16),
            pltpu.VMEM((NS, 2, 3, RS, HALF), BF16),
            pltpu.SemaphoreType.DMA((5,)),
            pltpu.SemaphoreType.DMA((n_sem,)),
            pltpu.SemaphoreType.DMA((NS + 5,)),
        ],
        compiler_params=pltpu.CompilerParams(
            collective_id=0, has_side_effects=True, vmem_limit_bytes=67043328
        ),
    )(
        tokens.reshape(2, 2, NS, RS, KC),
        query_weight,
        down,
        up.reshape(64, 16384),
        request_combination.reshape(1, 2048),
        task_ids.T,
        coefficient.T,
    )


def solution(mesh):
    placed = (
        P("tensor", "adapter"),
        P("adapter", "tensor"),
        P("adapter", None, None),
        P("adapter", None, None),
        P(),
        P(),
        P(),
    )
    return jax.shard_map(
        body, mesh=mesh, in_specs=placed, out_specs=P("adapter", "tensor"), check_vma=False
    )
```
